32 devices in a mesh: tm: 8 (over z, core), trans: 4 (over y, x).
Axes of the slice: x: 2, y: 2, z: 4, core: 2. Of those that a mesh axis runs over, the one named last changes fastest.
Arguments:
- light_field: float32 [2, 256, 16, 1024], P(None, 'trans', 'tm'), may hold values from -6 to 6
- gas_density: float32 [256, 1024], replicated, may hold values from 0.5 to 2
- phase_x: float32 [256], replicated, may hold values from -3.140625 to 3.140625
- phase_y: float32 [1024], replicated, may hold values from -3.140625 to 3.140625
Outputs:
- light_out: float32 [2, 256, 16, 1024], P(None, 'trans', 'tm')
- electrons: float32 [256, 16, 1024], P('trans', 'tm')
The draws below stay inside these ranges and needn't reach their ends.
All inputs are finite; a program needn't handle non-finite values.
Results may differ from the reference program's by a relative error of at most 0.0003.
Values sent between devices are 32-bit elements; how exact they have to be, the bound alone decides.
No kernel may reach another device: no remote copies, remote signals or barrier semaphores. Data moves between devices by JAX's collectives and lax.ppermute only.
A program may use at most 64 MiB of HBM per device.

```python
import math
import jax
import jax.numpy as jnp
from jax import lax

NX = 256
NY = 1024
PHOTONS = 8
STEPS = 2
NT = 16


def shard_levels(key, dims, cuts, smallest, top_value):
    def one(dim, shards_of):
        steps = jax.random.uniform(jax.random.fold_in(jax.random.fold_in(key, 6), dim), (shards_of,), jnp.float32, smallest / len(cuts), top_value / len(cuts))
        return jnp.repeat(jnp.exp(steps), dims[dim] // shards_of).reshape((-1,) + (1,) * (len(dims) - dim - 1))

    gain = one(*cuts[0])
    for cut in cuts[1:]:
        gain = gain * one(*cut)
    return gain


def gaussian(stream_key, shape, deviation, bound, split=(), kind=jnp.bfloat16):
    gain = shard_levels(stream_key, shape, split, -0.22, 0.18) if split else 1.0
    result = jax.random.normal(stream_key, shape, jnp.float32) * deviation * gain
    return jnp.minimum(jnp.maximum(result, -bound), bound).astype(kind)


def setup_inputs(seed: int = 0) -> dict:
    key_of = jax.random.split(jax.random.key(seed), 5)
    return {
        "light_field": gaussian(key_of[0], (2, NX, NT, NY), 1.0, 6.0, ((1, 4), (2, 8)), jnp.float32),
        "gas_density": jnp.clip(jnp.exp(jax.random.uniform(key_of[1], (NX, NY), jnp.float32, math.log(0.5), math.log(2.0))), 0.5, 2.0),
        "phase_x": jnp.clip(jax.random.uniform(key_of[2], (NX,), jnp.float32, -3.140625, 3.140625), -3.140625, 3.140625),
        "phase_y": jnp.clip(jax.random.uniform(key_of[3], (NY,), jnp.float32, -3.140625, 3.140625), -3.140625, 3.140625),
    }


RATE_COEF = 1.8e-8
RECOMB = 0.02
KERR_COEF = 0.3
PLASMA = 4.0


def nonlinear(complex_wave, gas_density):
    intensity = jnp.real(complex_wave) ** 2 + jnp.imag(complex_wave) ** 2
    ion_rate = RATE_COEF * intensity ** PHOTONS
    decays = jnp.exp(-(ion_rate + RECOMB))
    source = (1.0 - decays) * gas_density[:, None, :] * ion_rate / (ion_rate + RECOMB)

    def advance(carried, pieces):
        updated = pieces[0] * carried + pieces[1]
        return updated, updated

    start = jnp.zeros((intensity.shape[0], intensity.shape[2]), dtype=intensity.dtype)
    _, stacked = lax.scan(advance, start, (jnp.moveaxis(decays, 1, 0), jnp.moveaxis(source, 1, 0)))
    electrons = jnp.moveaxis(stacked, 0, 1)
    phase_shift = KERR_COEF * intensity - PLASMA * electrons
    return complex_wave * jnp.exp(1j * phase_shift), electrons


def reference(light_field, gas_density, phase_x, phase_y):
    complex_wave = light_field[0] + 1j * light_field[1]
    electrons = jnp.zeros(light_field.shape[1:], dtype=jnp.float32)
    for turn_index in range(STEPS):
        spectrum = jnp.fft.fft(complex_wave, axis=2) * jnp.exp(1j * phase_y)
        complex_wave = jnp.fft.ifft(spectrum, axis=2)
        spectrum = jnp.fft.fft(complex_wave, axis=0) * jnp.exp(1j * phase_x)[:, None, None]
        complex_wave = jnp.fft.ifft(spectrum, axis=0)
        complex_wave, electrons = nonlinear(complex_wave, gas_density)
    return jnp.stack([jnp.real(complex_wave), jnp.imag(complex_wave)]), electrons
```

```python
import functools
import math

import jax
import jax.numpy as jnp
import numpy as np
from jax import lax
from jax.experimental import pallas as pl
from jax.experimental.pallas import tpu as pltpu
from jax.sharding import Mesh
from jax.sharding import PartitionSpec as P

PHOTONS = 8
STEPS = 2
RATE_COEF = 1.8e-08
RECOMB = 0.02
KERR_COEF = 0.3
PLASMA = 4.0
LANES = 128
F32 = jnp.float32
BF16 = jnp.bfloat16
VMEM_SPEC = pl.BlockSpec(memory_space=pltpu.VMEM)
SMEM_SPEC = pl.BlockSpec(memory_space=pltpu.SMEM)


def sincos(angle):
    turns = jnp.floor(angle * (2.0 / math.pi) + 0.5)
    rest = angle - turns * 1.5703125
    rest = rest - turns * 4.837512969970703125e-4
    rest = rest - turns * 7.54978995489188e-8
    square = rest * rest
    sine = ((-1.9515295891e-4 * square + 8.3321608736e-3) * square - 1.6666654611e-1) * square
    sine = sine * rest + rest
    cosine = (2.443315711809948e-5 * square - 1.388731625493765e-3) * square
    cosine = (cosine + 4.166664568298827e-2) * (square * square) - 0.5 * square + 1.0
    quadrant = turns.astype(jnp.int32)
    odd = (quadrant & 1) == 1
    sine, cosine = jnp.where(odd, cosine, sine), jnp.where(odd, sine, cosine)
    sine = jnp.where((quadrant & 2) == 2, -sine, sine)
    cosine = jnp.where(((quadrant + 1) & 2) == 2, -cosine, cosine)
    return sine, cosine


def split3(value):
    high = value.astype(BF16)
    rest = value - high.astype(F32)
    middle = rest.astype(BF16)
    low = (rest - middle.astype(F32)).astype(BF16)
    return high, middle, low


def turned(value, order, position, sign):
    re, im = value
    eighth = (position * 8) // order
    if (position * 8) % order == 0 and eighth % 2 == 0:
        quarter = (eighth // 2 * sign) % 4
        return ((re, im), (-im, re), (-re, -im), (im, -re))[quarter]
    angle = sign * 2.0 * math.pi * position / order
    c, s = math.cos(angle), math.sin(angle)
    if (position * 8) % order == 0:
        root = math.sqrt(0.5)
        sc, ss = math.copysign(1, c), math.copysign(1, s)
        one = re - im if sc == ss else re + im
        two = re + im if sc == ss else re - im
        new_re = one * (root * sc)
        new_im = two * (root * ss) if sc == ss else two * (root * ss)
        return (new_re, new_im)
    return (re * c - im * s, re * s + im * c)


def small_dft(values, sign):
    count = len(values)
    if count == 1:
        return values
    even = small_dft(values[0::2], sign)
    odd = small_dft(values[1::2], sign)
    upper, lower = [], []
    for k in range(count // 2):
        other = turned(odd[k], count, k, sign)
        upper.append((even[k][0] + other[0], even[k][1] + other[1]))
        lower.append((even[k][0] - other[0], even[k][1] - other[1]))
    return upper + lower


def ionise(re, im, density):
    intensity = re * re + im * im
    power = intensity * intensity
    power = power * power
    rate = RATE_COEF * (power * power)
    loss = rate + RECOMB
    decay = jnp.exp(-loss)
    source = (1.0 - decay) * density * rate / loss
    return decay, source


def rotate(re, im, electrons):
    intensity = re * re + im * im
    sine, cosine = sincos(KERR_COEF * intensity - PLASMA * electrons)
    return re * cosine - im * sine, re * sine + im * cosine


def phase_tables(radix, sign):
    length = radix * LANES
    low = np.arange(LANES)
    angle = 2.0 * np.pi * (np.outer(low, low) % length) / length
    waves = np.concatenate([np.cos(angle), sign * np.sin(angle)], axis=1)
    block = 2.0 * np.pi * (np.outer(np.arange(radix), low) % radix) / radix
    turns = np.stack([np.cos(block), sign * np.sin(block)]) / length
    return waves.astype(np.float32), turns.astype(np.float32)


def toeplitz_blocks(phase, waves, turns, radix, sign):
    sine, cosine = sincos(phase)
    lane = lax.broadcasted_iota(jnp.int32, phase.shape, 1) % radix
    picked = [jnp.where(lane == k, part, 0.0) for part in (cosine, sine) for k in range(radix)]
    stacked = jnp.concatenate(picked, axis=0)
    spectrum = jnp.dot(
        stacked, waves, precision=lax.Precision.HIGHEST, preferred_element_type=F32
    )
    half = radix * radix
    row = lax.broadcasted_iota(jnp.int32, (LANES, LANES), 0)
    column = lax.broadcasted_iota(jnp.int32, (LANES, LANES), 1)
    blocks = []
    for k in range(radix):
        ours = slice(k * radix, (k + 1) * radix)
        theirs = slice(half + k * radix, half + (k + 1) * radix)
        re = spectrum[ours, :LANES] - spectrum[theirs, LANES:]
        im = spectrum[ours, LANES:] + spectrum[theirs, :LANES]
        full_re = jnp.sum(re * turns[0] - im * turns[1], axis=0, keepdims=True)
        full_im = jnp.sum(re * turns[1] + im * turns[0], axis=0, keepdims=True)
        spread_re = jnp.broadcast_to(full_re, (LANES, LANES))
        spread_im = jnp.broadcast_to(full_im, (LANES, LANES))
        rolled = (
            pltpu.roll(spread_re, 0, 1, stride=1, stride_axis=0),
            pltpu.roll(spread_im, 0, 1, stride=1, stride_axis=0),
        )
        wrapped = turned(rolled, radix, k, -sign)
        direct = column >= row
        blocks.append(
            (jnp.where(direct, rolled[0], wrapped[0]), jnp.where(direct, rolled[1], wrapped[1]))
        )
    return blocks


def store_right(table_ref, k, block):
    for part, (re, im) in enumerate(zip(split3(block[0]), split3(block[1]), strict=True)):
        base = part * 2 * LANES
        table_ref[k, base : base + LANES, :LANES] = re
        table_ref[k, base : base + LANES, LANES:] = im
        table_ref[k, base + LANES : base + 2 * LANES, :LANES] = -im
        table_ref[k, base + LANES : base + 2 * LANES, LANES:] = re


def store_left(table_ref, k, block):
    for part, (re, im) in enumerate(zip(split3(block[0]), split3(block[1]), strict=True)):
        base = part * 2 * LANES
        table_ref[k, :LANES, base : base + LANES] = re
        table_ref[k, LANES:, base : base + LANES] = im
        table_ref[k, :LANES, base + LANES : base + 2 * LANES] = -im
        table_ref[k, LANES:, base + LANES : base + 2 * LANES] = re


def forward_y(load, rows, radix, parts_ref):
    step = min(16, rows)
    for start in range(0, rows, step):
        blocks = small_dft([load(start, step, a) for a in range(radix)], -1)
        for k, (re, im) in enumerate(blocks):
            for part, (a, b) in enumerate(zip(split3(re), split3(im), strict=True)):
                parts_ref[k, part, start : start + step, :LANES] = a
                parts_ref[k, part, start : start + step, LANES:] = b


def product_y(parts_ref, table_ref, out_ref, radix):
    for k in range(radix):
        high, middle, low = parts_ref[k, 0], parts_ref[k, 1], parts_ref[k, 2]
        left = jnp.concatenate([high, high, high, middle, middle, low], axis=1)
        table = table_ref[k]
        right = jnp.concatenate([table, table[: 4 * LANES], table[: 2 * LANES]], axis=0)
        out_ref[k] = jnp.dot(left, right, preferred_element_type=F32)


def backward_y(out_ref, start, step, radix):
    picked = [
        (out_ref[k, start : start + step, :LANES], out_ref[k, start : start + step, LANES:])
        for k in range(radix)
    ]
    return small_dft(picked, 1)


def first_kernel(light_ref, phase_ref, waves_ref, turns_ref, send_ref, table_ref, parts_ref, mid_ref):
    radix = table_ref.shape[0]
    slabs, _, times, across, width = send_ref.shape
    blocks = toeplitz_blocks(phase_ref[...], waves_ref[...], turns_ref[...], radix, 1)
    for k, block in enumerate(blocks):
        store_right(table_ref, k, block)

    def load(start, step, a):
        t, x = start // across, start % across
        lanes = slice(a * LANES, (a + 1) * LANES)
        return light_ref[0, t, x : x + step, lanes], light_ref[1, t, x : x + step, lanes]

    forward_y(load, times * across, radix, parts_ref)
    product_y(parts_ref, table_ref, mid_ref, radix)
    for start in range(0, times * across, 8):
        t, x = start // across, start % across
        for a, pair in enumerate(backward_y(mid_ref, start, 8, radix)):
            for c in range(2):
                if width >= LANES:
                    slab, offset = a * LANES // width, a * LANES % width
                    send_ref[slab, c, t, x : x + 8, offset : offset + LANES] = pair[c]
                else:
                    for piece in range(LANES // width):
                        slab = a * LANES // width + piece
                        send_ref[slab, c, t, x : x + 8, :] = pair[c][
                            :, piece * width : (piece + 1) * width
                        ]


def table_x_kernel(phase_ref, waves_ref, turns_ref, table_ref):
    radix = table_ref.shape[0]
    blocks = toeplitz_blocks(phase_ref[...], waves_ref[...], turns_ref[...], radix, -1)
    for k, block in enumerate(blocks):
        store_left(table_ref, k, block)


def put_x(parts_ref, lanes, start, values):
    step = values[0][0].shape[0]
    for k, (re, im) in enumerate(small_dft(values, -1)):
        for part, (a, b) in enumerate(zip(split3(re), split3(im), strict=True)):
            base = part * 2 * LANES
            parts_ref[k, base + start : base + start + step, lanes] = a
            parts_ref[k, base + LANES + start : base + LANES + start + step, lanes] = b


def product_x(parts_ref, table_ref, out_ref, radix):
    for k in range(radix):
        table = table_ref[k]
        left = jnp.concatenate([table, table[:, : 4 * LANES], table[:, : 2 * LANES]], axis=1)
        high = parts_ref[k, : 2 * LANES]
        middle = parts_ref[k, 2 * LANES : 4 * LANES]
        low = parts_ref[k, 4 * LANES :]
        right = jnp.concatenate([high, high, high, middle, middle, low], axis=0)
        out_ref[k] = jnp.dot(left, right, preferred_element_type=F32)


def get_x(out_ref, lanes, start, step, radix):
    picked = [
        (out_ref[k, start : start + step, lanes], out_ref[k, LANES + start : LANES + start + step, lanes])
        for k in range(radix)
    ]
    return small_dft(picked, 1)


def second_kernel(
    recv_ref, table_ref, density_ref, field_ref, growth_ref, gained_ref, last_growth_ref, last_gained_ref,
    parts_ref, mid_ref,
):
    radix = table_ref.shape[0]
    sources, _, times, across, width = recv_ref.shape
    trans = (radix * LANES) // across
    step = min(16, across)
    total = (sources // trans) * times

    def at(c, t, x):
        core, inner = t // times, t % times
        return recv_ref[core * trans + x // across, c, inner, x % across : x % across + step, :]

    for t in range(total):
        lanes = slice(t * width, (t + 1) * width)
        for start in range(0, LANES, step):
            values = [
                (at(0, t, a * LANES + start), at(1, t, a * LANES + start)) for a in range(radix)
            ]
            put_x(parts_ref, lanes, start, values)
    product_x(parts_ref, table_ref, mid_ref, radix)
    for start in range(0, LANES, 8):
        growth, gained = [None] * radix, [None] * radix
        for t in range(total):
            lanes = slice(t * width, (t + 1) * width)
            for a, (re, im) in enumerate(get_x(mid_ref, lanes, start, 8, radix)):
                rows = slice(a * LANES + start, a * LANES + start + 8)
                field_ref[0, t, rows, :] = re
                field_ref[1, t, rows, :] = im
                decay, source = ionise(re, im, density_ref[rows, :])
                if t == 0:
                    growth[a], gained[a] = decay, source
                else:
                    gained[a] = decay * gained[a] + source
                    growth[a] = growth[a] * decay
                growth_ref[t, rows, :] = growth[a]
                gained_ref[t, rows, :] = gained[a]
                if t == total - 1:
                    last_growth_ref[rows, :] = growth[a]
                    last_gained_ref[rows, :] = gained[a]


def third_kernel(
    field_ref, growth_ref, gained_ref, entering_ref, table_ref, send_ref, parts_ref, mid_ref
):
    radix = table_ref.shape[0]
    _, total, _, width = field_ref.shape
    slabs, _, times, across, _ = send_ref.shape
    trans = (radix * LANES) // across
    for t in range(total):
        lanes = slice(t * width, (t + 1) * width)
        for start in range(0, LANES, 16):
            values = []
            for a in range(radix):
                rows = slice(a * LANES + start, a * LANES + start + 16)
                electrons = growth_ref[t, rows, :] * entering_ref[rows, :] + gained_ref[t, rows, :]
                values.append(rotate(field_ref[0, t, rows, :], field_ref[1, t, rows, :], electrons))
            put_x(parts_ref, lanes, start, values)
    product_x(parts_ref, table_ref, mid_ref, radix)
    for t in range(total):
        lanes = slice(t * width, (t + 1) * width)
        for start in range(0, LANES, 8):
            for a, pair in enumerate(get_x(mid_ref, lanes, start, 8, radix)):
                x = a * LANES + start
                slab = (t // times) * trans + x // across
                row = x % across
                for c in range(2):
                    send_ref[slab, c, t % times, row : row + 8, :] = pair[c]


def fourth_kernel(
    core_ref, recv_ref, table_ref, density_ref, field_ref, growth_ref, gained_ref, mine_ref, theirs_ref,
    parts_ref, mid_ref,
):
    radix = table_ref.shape[0]
    slabs, _, times, across, width = recv_ref.shape
    core = core_ref[0]

    def part(c, t, x, step, a):
        if width >= LANES:
            slab, offset = a * LANES // width, a * LANES % width
            return recv_ref[slab, c, t, x : x + step, offset : offset + LANES]
        pieces = LANES // width
        return jnp.concatenate(
            [recv_ref[a * pieces + p, c, t, x : x + step, :] for p in range(pieces)], axis=1
        )

    def load(start, step, a):
        t, x = start // across, start % across
        return part(0, t, x, step, a), part(1, t, x, step, a)

    forward_y(load, times * across, radix, parts_ref)
    product_y(parts_ref, table_ref, mid_ref, radix)
    half = across // 2
    for x in range(0, across, 8):
        growth, gained = [None] * radix, [None] * radix
        for t in range(times):
            for a, (re, im) in enumerate(backward_y(mid_ref, t * across + x, 8, radix)):
                lanes = slice(a * LANES, (a + 1) * LANES)
                field_ref[0, t, x : x + 8, lanes] = re
                field_ref[1, t, x : x + 8, lanes] = im
                decay, source = ionise(re, im, density_ref[x : x + 8, lanes])
                if t == 0:
                    growth[a], gained[a] = decay, source
                else:
                    gained[a] = decay * gained[a] + source
                    growth[a] = growth[a] * decay
                growth_ref[t, x : x + 8, lanes] = growth[a]
                gained_ref[t, x : x + 8, lanes] = gained[a]
    last = times - 1

    def hand_out(own):
        kept, given = slice(own * half, (own + 1) * half), slice((1 - own) * half, (2 - own) * half)
        mine_ref[0] = growth_ref[last, kept, :]
        mine_ref[1] = gained_ref[last, kept, :]
        theirs_ref[0] = growth_ref[last, given, :]
        theirs_ref[1] = gained_ref[last, given, :]

    pl.when(core == 0)(functools.partial(hand_out, 0))
    pl.when(core == 1)(functools.partial(hand_out, 1))


def fifth_kernel(core_ref, field_ref, growth_ref, gained_ref, kept_ref, given_ref, light_ref, electrons_ref):
    _, times, across, length = field_ref.shape
    half = across // 2
    core = core_ref[0]
    for x in range(0, across, 8):
        own, row = x // half, x % half
        entering = jnp.where(core == own, kept_ref[row : row + 8, :], given_ref[row : row + 8, :])
        for t in range(times):
            for a in range(length // LANES):
                lanes = slice(a * LANES, (a + 1) * LANES)
                electrons = (
                    growth_ref[t, x : x + 8, lanes] * entering[:, lanes]
                    + gained_ref[t, x : x + 8, lanes]
                )
                re, im = rotate(
                    field_ref[0, t, x : x + 8, lanes], field_ref[1, t, x : x + 8, lanes], electrons
                )
                light_ref[0, t, x : x + 8, lanes] = re
                light_ref[1, t, x : x + 8, lanes] = im
                electrons_ref[t, x : x + 8, lanes] = electrons


def call(kernel, outs, scratch, *operands, scalars=0):
    return pl.pallas_call(
        kernel,
        out_shape=[jax.ShapeDtypeStruct(shape, kind) for shape, kind in outs],
        in_specs=[SMEM_SPEC] * scalars + [VMEM_SPEC] * (len(operands) - scalars),
        out_specs=[VMEM_SPEC] * len(outs),
        scratch_shapes=[pltpu.VMEM(shape, kind) for shape, kind in scratch],
    )(*operands)


def entering_chip(growth, gained):
    count = lax.axis_size("z")
    place = lax.axis_index("z")
    before_growth = before_gained = None
    size = 1
    while size < count:
        got_growth = jnp.zeros_like(growth)
        got_gained = jnp.zeros_like(gained)
        need_growth = 2 * size < count
        for reach in range(1, size + 1):
            pairs = [
                (b + size - 1, b + size - 1 + reach)
                for b in range(0, count, 2 * size)
                if b + size - 1 + reach < count
            ]
            got_gained = got_gained + lax.ppermute(gained, "z", pairs)
            if need_growth:
                later = [pair for pair in pairs if pair[0] >= 2 * size]
                got_growth = got_growth + lax.ppermute(growth, "z", later)
        upper = (place // size) % 2 == 1
        if before_gained is None:
            new_gained, new_growth = got_gained, got_growth
            before_gained = jnp.zeros_like(gained)
            before_growth = jnp.ones_like(growth)
        else:
            new_gained = before_growth * got_gained + before_gained
            new_growth = before_growth * got_growth
        before_gained = jnp.where(upper, new_gained, before_gained)
        if need_growth:
            before_growth = jnp.where(upper, new_growth, before_growth)
            gained, growth = (
                jnp.where(upper, growth * got_gained + gained, gained),
                jnp.where(upper, growth * got_growth, growth),
            )
        size *= 2
    return jnp.zeros_like(gained) if before_gained is None else before_gained


def local(light_field, gas_density, phase_x, phase_y):
    width_x, width_y = phase_x.shape[0], phase_y.shape[0]
    radix_x, radix_y = width_x // LANES, width_y // LANES
    _, across, times, _ = light_field.shape
    trans, cores = lax.axis_size("trans"), lax.axis_size("core")
    slabs = trans * cores
    width = width_y // slabs
    total = times * cores
    slab = lax.axis_index("core") * trans + lax.axis_index("trans")
    core = lax.axis_index("core").astype(jnp.int32).reshape(1)
    density_y = lax.dynamic_slice_in_dim(gas_density, slab * width, width, 1)
    density_x = lax.dynamic_slice_in_dim(gas_density, lax.axis_index("trans") * across, across, 0)
    packed = (slabs, 2, times, across, width)
    rows = times * across

    waves_y, turns_y = phase_tables(radix_y, 1)
    waves_x, turns_x = phase_tables(radix_x, -1)
    scratch_y = [((radix_y, 3, rows, 2 * LANES), BF16), ((radix_y, rows, 2 * LANES), F32)]
    scratch_x = [
        ((radix_x, 6 * LANES, total * width), BF16),
        ((radix_x, 2 * LANES, total * width), F32),
    ]
    (table_x,) = call(
        table_x_kernel,
        [((radix_x, 2 * LANES, 6 * LANES), BF16)],
        [],
        phase_x.reshape(radix_x, LANES),
        waves_x,
        turns_x,
    )
    sent, table_y = call(
        first_kernel,
        [(packed, F32), ((radix_y, 6 * LANES, 2 * LANES), BF16)],
        scratch_y,
        light_field.transpose(0, 2, 1, 3),
        phase_y.reshape(radix_y, LANES),
        waves_y,
        turns_y,
    )
    received = lax.all_to_all(sent, ("core", "trans"), 0, 0, tiled=True)
    cells = (width_x, width)
    field, growth, gained, last_growth, last_gained = call(
        second_kernel,
        [((2, total) + cells, F32), ((total,) + cells, F32), ((total,) + cells, F32), (cells, F32), (cells, F32)],
        scratch_x,
        received,
        table_x,
        density_y,
    )
    entering = entering_chip(last_growth, last_gained)
    (sent,) = call(
        third_kernel, [(packed, F32)], scratch_x, field, growth, gained, entering, table_x
    )
    received = lax.all_to_all(sent, ("core", "trans"), 0, 0, tiled=True)
    cells = (across, width_y)
    half = (2, across // 2, width_y)
    field, growth, gained, mine, theirs = call(
        fourth_kernel,
        [((2, times) + cells, F32), ((times,) + cells, F32), ((times,) + cells, F32), (half, F32), (half, F32)],
        scratch_y,
        core,
        received,
        table_y,
        density_x,
        scalars=1,
    )
    swap = [(0, 1), (1, 0)]
    other = lax.ppermute(theirs, "core", swap)
    first = core[0] == 0
    early = jnp.where(first, mine, other)
    late = jnp.where(first, other, mine)
    entering = entering_chip(late[0] * early[0], late[0] * early[1] + late[1])
    halfway = early[0] * entering + early[1]
    kept = jnp.where(first, entering, halfway)
    given = lax.ppermute(jnp.where(first, halfway, entering), "core", swap)
    light, electrons = call(
        fifth_kernel,
        [((2, times) + cells, F32), ((times,) + cells, F32)],
        [],
        core,
        field,
        growth,
        gained,
        kept,
        given,
        scalars=1,
    )
    return light.transpose(0, 2, 1, 3), electrons.transpose(1, 0, 2)


def solution(mesh):
    count = mesh.shape["tm"]
    split = Mesh(
        mesh.devices.reshape(count // 2, 2, mesh.shape["trans"]), ("z", "core", "trans")
    )
    placed = (P(None, "trans", ("z", "core"), None), P(), P(), P())
    return jax.shard_map(
        local,
        mesh=split,
        in_specs=placed,
        out_specs=(P(None, "trans", ("z", "core"), None), P("trans", ("z", "core"), None)),
        check_vma=False,
    )
```

```python
import functools
import math

import jax
import jax.numpy as jnp
from jax import lax
from jax.experimental import pallas as pl
from jax.experimental.pallas import tpu as pltpu
from jax.sharding import Mesh
from jax.sharding import PartitionSpec as P

PHOTONS = 8
STEPS = 2
RATE_COEF = 1.8e-08
RECOMB = 0.02
KERR_COEF = 0.3
PLASMA = 4.0
LANES = 128
HALF = LANES // 2
VMEM_LIMIT = 16 * 1024 * 1024
F32 = jnp.float32
BF16 = jnp.bfloat16
VMEM_SPEC = pl.BlockSpec(memory_space=pltpu.VMEM)
ANY_SPEC = pl.BlockSpec(memory_space=pl.ANY)
HBM_SPEC = pl.BlockSpec(memory_space=pltpu.MemorySpace.HBM)


def sincos(angle):
    turns = jnp.floor(angle * (2.0 / math.pi) + 0.5)
    rest = angle - turns * 1.5703125
    rest = rest - turns * 4.837512969970703125e-4
    rest = rest - turns * 7.54978995489188e-8
    square = rest * rest
    sine = ((-1.9515295891e-4 * square + 8.3321608736e-3) * square - 1.6666654611e-1) * square
    sine = sine * rest + rest
    cosine = (2.443315711809948e-5 * square - 1.388731625493765e-3) * square
    cosine = (cosine + 4.166664568298827e-2) * (square * square) - 0.5 * square + 1.0
    quadrant = turns.astype(jnp.int32)
    odd = (quadrant & 1) == 1
    sine, cosine = jnp.where(odd, cosine, sine), jnp.where(odd, sine, cosine)
    sine = jnp.where((quadrant & 2) == 2, -sine, sine)
    cosine = jnp.where(((quadrant + 1) & 2) == 2, -cosine, cosine)
    return sine, cosine


def split3(value):
    high = value.astype(BF16)
    rest = value - high.astype(F32)
    middle = rest.astype(BF16)
    low = (rest - middle.astype(F32)).astype(BF16)
    return high, middle, low


def turned(value, order, position, sign):
    re, im = value
    eighth = (position * 8) // order
    if (position * 8) % order == 0 and eighth % 2 == 0:
        quarter = (eighth // 2 * sign) % 4
        return ((re, im), (-im, re), (-re, -im), (im, -re))[quarter]
    angle = sign * 2.0 * math.pi * position / order
    c, s = math.cos(angle), math.sin(angle)
    if (position * 8) % order == 0:
        root = math.sqrt(0.5)
        sc, ss = math.copysign(1, c), math.copysign(1, s)
        one = re - im if sc == ss else re + im
        two = re + im if sc == ss else re - im
        new_re = one * (root * sc)
        new_im = two * (root * ss) if sc == ss else two * (root * ss)
        return (new_re, new_im)
    return (re * c - im * s, re * s + im * c)


def small_dft(values, sign):
    count = len(values)
    if count == 1:
        return values
    even = small_dft(values[0::2], sign)
    odd = small_dft(values[1::2], sign)
    upper, lower = [], []
    for k in range(count // 2):
        other = turned(odd[k], count, k, sign)
        upper.append((even[k][0] + other[0], even[k][1] + other[1]))
        lower.append((even[k][0] - other[0], even[k][1] - other[1]))
    return upper + lower


def ionise(re, im, density):
    intensity = re * re + im * im
    power = intensity * intensity
    power = power * power
    rate = RATE_COEF * (power * power)
    loss = rate + RECOMB
    decay = jnp.exp(-loss)
    source = (1.0 - decay) * density * rate / loss
    return decay, source


def rotate(re, im, electrons):
    intensity = re * re + im * im
    sine, cosine = sincos(KERR_COEF * intensity - PLASMA * electrons)
    return re * cosine - im * sine, re * sine + im * cosine


def wave(shape, order, sign):
    product = lax.broadcasted_iota(jnp.int32, shape, 0) * lax.broadcasted_iota(jnp.int32, shape, 1)
    sine, cosine = sincos((product % order).astype(F32) * (2.0 * math.pi / order))
    return cosine, sign * sine


def toeplitz_blocks(phase, radix, sign):
    length = radix * LANES
    waves = jnp.concatenate(wave((LANES, LANES), length, sign), axis=1)
    block_re, block_im = wave((radix, LANES), radix, sign)
    block_re, block_im = block_re * (1.0 / length), block_im * (1.0 / length)
    sine, cosine = sincos(phase)
    lane = lax.broadcasted_iota(jnp.int32, phase.shape, 1) % radix
    picked = [jnp.where(lane == k, part, 0.0) for part in (cosine, sine) for k in range(radix)]
    spectrum = jnp.dot(
        jnp.concatenate(picked, axis=0),
        waves,
        precision=lax.Precision.HIGHEST,
        preferred_element_type=F32,
    )
    half = radix * radix
    row = lax.broadcasted_iota(jnp.int32, (LANES, LANES), 0)
    column = lax.broadcasted_iota(jnp.int32, (LANES, LANES), 1)
    direct = column >= row
    blocks = []
    for k in range(radix):
        ours = slice(k * radix, (k + 1) * radix)
        theirs = slice(half + k * radix, half + (k + 1) * radix)
        re = spectrum[ours, :LANES] - spectrum[theirs, LANES:]
        im = spectrum[ours, LANES:] + spectrum[theirs, :LANES]
        full_re = jnp.sum(re * block_re - im * block_im, axis=0, keepdims=True)
        full_im = jnp.sum(re * block_im + im * block_re, axis=0, keepdims=True)
        spread_re = jnp.broadcast_to(full_re, (LANES, LANES))
        spread_im = jnp.broadcast_to(full_im, (LANES, LANES))
        rolled = (
            pltpu.roll(spread_re, 0, 1, stride=1, stride_axis=0),
            pltpu.roll(spread_im, 0, 1, stride=1, stride_axis=0),
        )
        wrapped = turned(rolled, radix, k, -sign)
        blocks.append(
            (jnp.where(direct, rolled[0], wrapped[0]), jnp.where(direct, rolled[1], wrapped[1]))
        )
    return blocks


def store_parts(table_ref, blocks):
    for k, (re, im) in enumerate(blocks):
        for part, (a, b) in enumerate(zip(split3(re), split3(im), strict=True)):
            table_ref[k, part, 0] = a
            table_ref[k, part, 1] = b


def table_kernel(sign, phase_ref, *refs):
    table_ref = refs[-1]
    store_parts(table_ref, toeplitz_blocks(phase_ref[...], table_ref.shape[0], sign))


def forward_y(load, start, step, radix, parts_ref):
    blocks = small_dft([load(a) for a in range(radix)], -1)
    for k, (re, im) in enumerate(blocks):
        for part, (a, b) in enumerate(zip(split3(re), split3(im), strict=True)):
            parts_ref[k, part, start : start + step, :LANES] = a
            parts_ref[k, part, start : start + step, LANES:] = b


def product_y(parts_ref, table_ref, out_ref, radix):
    for k in range(radix):
        high, middle, low = parts_ref[k, 0], parts_ref[k, 1], parts_ref[k, 2]
        left = jnp.concatenate([high, high, high, middle, middle, low], axis=1)
        rights = []
        for part in range(3):
            re, im = table_ref[k, part, 0], table_ref[k, part, 1]
            rights.append(jnp.concatenate([re, im], axis=1))
            rights.append(jnp.concatenate([-im, re], axis=1))
        right = jnp.concatenate(rights + rights[:4] + rights[:2], axis=0)
        out_ref[k] = jnp.dot(left, right, preferred_element_type=F32)


def backward_y(out_ref, start, step, radix):
    picked = [
        (out_ref[k, start : start + step, :LANES], out_ref[k, start : start + step, LANES:])
        for k in range(radix)
    ]
    return small_dft(picked, 1)


def upper_lanes(shape):
    return lax.broadcasted_iota(jnp.int32, shape, 1) >= HALF


def swap_halves(value):
    return pltpu.roll(value, HALF, 1)


def first_kernel(
    packed, light_hbm, phase_hbm, send_hbm, table_ref, parts_ref, mid_ref, light_ref, phase_ref, send_ref, sem
):
    radix = table_ref.shape[0]
    _, across, times, _ = light_ref.shape
    width = send_ref.shape[-1]
    step = min(16, across)
    chunks = range(0, across, step)
    phase_copy = pltpu.make_async_copy(phase_hbm, phase_ref, sem.at[0])
    phase_copy.start()
    arriving = []
    for i, x in enumerate(chunks):
        rows = pl.ds(x, step)
        copy = pltpu.make_async_copy(light_hbm.at[:, rows], light_ref.at[:, rows], sem.at[1 + i])
        copy.start()
        arriving.append(copy)
    phase_copy.wait()
    store_parts(table_ref, toeplitz_blocks(phase_ref[...], radix, 1))
    for copy, x in zip(arriving, chunks, strict=True):
        copy.wait()
        for t in range(times):

            def load(a, x=x, t=t):
                lanes = slice(a * LANES, (a + 1) * LANES)
                rows = slice(x, x + step)
                return light_ref[0, rows, t, lanes], light_ref[1, rows, t, lanes]

            forward_y(load, t * across + x, step, radix, parts_ref)
    product_y(parts_ref, table_ref, mid_ref, radix)
    leaving = []
    upper = upper_lanes((8, LANES))
    for i, begin in enumerate(chunks):
        for x in range(begin, begin + step, 8):
            rows = slice(x, x + 8)
            results = [backward_y(mid_ref, t * across + x, 8, radix) for t in range(times)]
            for a in range(radix):
                for c in range(2):
                    values = [results[t][a][c] for t in range(times)]
                    if packed:
                        one, two = values
                        send_ref[2 * a, c, 0, rows, :] = jnp.where(upper, swap_halves(two), one)
                        send_ref[2 * a + 1, c, 0, rows, :] = jnp.where(upper, two, swap_halves(one))
                    elif width >= LANES:
                        slab, offset = a * LANES // width, a * LANES % width
                        for t in range(times):
                            send_ref[slab, c, t, rows, offset : offset + LANES] = values[t]
                    else:
                        for t in range(times):
                            for piece in range(LANES // width):
                                slab = a * LANES // width + piece
                                lanes = slice(piece * width, (piece + 1) * width)
                                send_ref[slab, c, t, rows, :] = values[t][:, lanes]
        rows = pl.ds(begin, step)
        copy = pltpu.make_async_copy(
            send_ref.at[:, :, :, rows], send_hbm.at[:, :, :, rows], sem.at[1 + i]
        )
        copy.start()
        leaving.append(copy)
    for copy in leaving:
        copy.wait()


def put_x(parts_ref, lanes, start, values):
    step = values[0][0].shape[0]
    for k, (re, im) in enumerate(small_dft(values, -1)):
        for part, (a, b) in enumerate(zip(split3(re), split3(im), strict=True)):
            base = part * 2 * LANES
            parts_ref[k, base + start : base + start + step, lanes] = a
            parts_ref[k, base + LANES + start : base + LANES + start + step, lanes] = b


def product_x(parts_ref, table_ref, out_ref, radix):
    for k in range(radix):
        lefts = []
        for part in range(3):
            re, im = table_ref[k, part, 0], table_ref[k, part, 1]
            lefts.append(jnp.concatenate([re, im], axis=0))
            lefts.append(jnp.concatenate([-im, re], axis=0))
        left = jnp.concatenate(lefts + lefts[:4] + lefts[:2], axis=1)
        high = parts_ref[k, : 2 * LANES]
        middle = parts_ref[k, 2 * LANES : 4 * LANES]
        low = parts_ref[k, 4 * LANES :]
        right = jnp.concatenate([high, high, high, middle, middle, low], axis=0)
        out_ref[k] = jnp.dot(left, right, preferred_element_type=F32)


def get_x(out_ref, lanes, start, step, radix):
    picked = [
        (out_ref[k, start : start + step, lanes], out_ref[k, LANES + start : LANES + start + step, lanes])
        for k in range(radix)
    ]
    return small_dft(picked, 1)


def second_kernel(
    packed, recv_ref, table_ref, density_ref, field_ref, growth_ref, gained_ref, last_growth_ref, last_gained_ref,
    parts_ref, mid_ref,
):
    radix = table_ref.shape[0]
    sources, _, times, across, width = recv_ref.shape
    trans = (radix * LANES) // across
    step = min(16, across)
    total = (sources // trans) * times

    def at(c, t, x):
        place, inner = t // times, t % times
        return recv_ref[place * trans + x // across, c, inner, x % across : x % across + step, :]

    for t in range(total):
        lanes = slice(t * width, (t + 1) * width)
        for start in range(0, LANES, step):
            values = [
                (at(0, t, a * LANES + start), at(1, t, a * LANES + start)) for a in range(radix)
            ]
            put_x(parts_ref, lanes, start, values)
    product_x(parts_ref, table_ref, mid_ref, radix)
    upper = upper_lanes((8, LANES))
    for start in range(0, LANES, 8):
        carry = [None] * radix
        for t in range(total):
            lanes = slice(t * width, (t + 1) * width)
            for a, (re, im) in enumerate(get_x(mid_ref, lanes, start, 8, radix)):
                rows = slice(a * LANES + start, a * LANES + start + 8)
                field_ref[0, t, rows, :] = re
                field_ref[1, t, rows, :] = im
                growth, gained = ionise(re, im, density_ref[rows, :])
                if packed:
                    gained = jnp.where(upper, growth * swap_halves(gained) + gained, gained)
                    growth = jnp.where(upper, growth * swap_halves(growth), growth)
                if carry[a] is not None:
                    gained = growth * carry[a][1] + gained
                    growth = growth * carry[a][0]
                growth_ref[t, rows, :] = growth
                gained_ref[t, rows, :] = gained
                if packed:
                    growth = jnp.where(upper, growth, swap_halves(growth))
                    gained = jnp.where(upper, gained, swap_halves(gained))
                carry[a] = (growth, gained)
        for a in range(radix // 2 if packed else radix):
            rows = slice(a * LANES + start, a * LANES + start + 8)
            growth, gained = carry[a]
            if packed:
                growth = jnp.where(upper, carry[a + radix // 2][0], growth)
                gained = jnp.where(upper, carry[a + radix // 2][1], gained)
            last_growth_ref[rows, :] = growth
            last_gained_ref[rows, :] = gained


def third_kernel(
    packed, field_ref, growth_ref, gained_ref, entering_ref, table_ref, send_hbm, token_ref,
    parts_ref, mid_ref, send_ref, sem,
):
    radix = table_ref.shape[0]
    _, total, _, width = field_ref.shape
    slabs, _, times, across, _ = send_ref.shape
    trans = (radix * LANES) // across
    token_ref[...] = jnp.zeros_like(token_ref)
    step = 16
    upper = upper_lanes((step, LANES))
    for start in range(0, LANES, step):
        entering = []
        for a in range(radix):
            if packed:
                base = (a % (radix // 2)) * LANES + start
                value = entering_ref[base : base + step, :]
                other = swap_halves(value)
                first = a < radix // 2
                entering.append(jnp.where(upper, other if first else value, value if first else other))
            else:
                entering.append(entering_ref[a * LANES + start : a * LANES + start + step, :])
        for t in range(total):
            lanes = slice(t * width, (t + 1) * width)
            values = []
            for a in range(radix):
                rows = slice(a * LANES + start, a * LANES + start + step)
                electrons = growth_ref[t, rows, :] * entering[a] + gained_ref[t, rows, :]
                values.append(rotate(field_ref[0, t, rows, :], field_ref[1, t, rows, :], electrons))
            put_x(parts_ref, lanes, start, values)
    product_x(parts_ref, table_ref, mid_ref, radix)
    leaving = []
    for t in range(total):
        lanes = slice(t * width, (t + 1) * width)
        place, inner = t // times, t % times
        for start in range(0, LANES, 8):
            for a, pair in enumerate(get_x(mid_ref, lanes, start, 8, radix)):
                x = a * LANES + start
                row = x % across
                for c in range(2):
                    send_ref[place * trans + x // across, c, inner, row : row + 8, :] = pair[c]
        if inner == times - 1:
            block = pl.ds(place * trans, trans)
            copy = pltpu.make_async_copy(send_ref.at[block], send_hbm.at[block], sem.at[place])
            copy.start()
            leaving.append(copy)
    for copy in leaving:
        copy.wait()


def fourth_kernel(
    packed, recv_ref, table_ref, density_ref, field_ref, growth_ref, gained_ref, mine_ref, theirs_ref,
    parts_ref, mid_ref,
):
    radix = table_ref.shape[0]
    _, times, across, _ = field_ref.shape
    width = recv_ref.shape[-1]
    core = lax.axis_index("core")
    step = min(16, across)
    upper = upper_lanes((step, LANES))

    def part(c, t, x, a):
        rows = slice(x, x + step)
        if packed:
            one, two = recv_ref[2 * a, c, 0, rows, :], recv_ref[2 * a + 1, c, 0, rows, :]
            if t == 0:
                return jnp.where(upper, swap_halves(two), one)
            return jnp.where(upper, two, swap_halves(one))
        if width >= LANES:
            slab, offset = a * LANES // width, a * LANES % width
            return recv_ref[slab, c, t, rows, offset : offset + LANES]
        pieces = LANES // width
        return jnp.concatenate(
            [recv_ref[a * pieces + p, c, t, rows, :] for p in range(pieces)], axis=1
        )

    for x in range(0, across, step):
        for t in range(times):

            def load(a, x=x, t=t):
                return part(0, t, x, a), part(1, t, x, a)

            forward_y(load, t * across + x, step, radix, parts_ref)
    product_y(parts_ref, table_ref, mid_ref, radix)
    half = across // 2
    for x in range(0, across, 8):
        rows = slice(x, x + 8)
        growth, gained = [None] * radix, [None] * radix
        for t in range(times):
            for a, (re, im) in enumerate(backward_y(mid_ref, t * across + x, 8, radix)):
                lanes = slice(a * LANES, (a + 1) * LANES)
                field_ref[0, t, rows, lanes] = re
                field_ref[1, t, rows, lanes] = im
                decay, source = ionise(re, im, density_ref[rows, lanes])
                if t == 0:
                    growth[a], gained[a] = decay, source
                else:
                    gained[a] = decay * gained[a] + source
                    growth[a] = growth[a] * decay
                growth_ref[t, rows, lanes] = growth[a]
                gained_ref[t, rows, lanes] = gained[a]
    last = times - 1

    def hand_out(own):
        kept, given = slice(own * half, (own + 1) * half), slice((1 - own) * half, (2 - own) * half)
        mine_ref[0] = growth_ref[last, kept, :]
        mine_ref[1] = gained_ref[last, kept, :]
        theirs_ref[0] = growth_ref[last, given, :]
        theirs_ref[1] = gained_ref[last, given, :]

    pl.when(core == 0)(functools.partial(hand_out, 0))
    pl.when(core == 1)(functools.partial(hand_out, 1))


def fifth_kernel(
    field_ref, growth_ref, gained_ref, kept_ref, given_ref, light_hbm, electrons_hbm, light_ref, electrons_ref, sem
):
    _, times, across, length = field_ref.shape
    half = across // 2
    core = lax.axis_index("core")
    step = min(16, half)
    leaving = []
    for i, begin in enumerate(range(0, across, step)):
        for x in range(begin, begin + step, 8):
            own, row = x // half, x % half
            rows = slice(x, x + 8)
            entering = jnp.where(core == own, kept_ref[row : row + 8, :], given_ref[row : row + 8, :])
            for t in range(times):
                for a in range(length // LANES):
                    lanes = slice(a * LANES, (a + 1) * LANES)
                    electrons = (
                        growth_ref[t, rows, lanes] * entering[:, lanes] + gained_ref[t, rows, lanes]
                    )
                    re, im = rotate(field_ref[0, t, rows, lanes], field_ref[1, t, rows, lanes], electrons)
                    light_ref[0, rows, t, lanes] = re
                    light_ref[1, rows, t, lanes] = im
                    electrons_ref[rows, t, lanes] = electrons
        block = pl.ds(begin, step)
        for copy in (
            pltpu.make_async_copy(light_ref.at[:, block], light_hbm.at[:, block], sem.at[0, i]),
            pltpu.make_async_copy(electrons_ref.at[block], electrons_hbm.at[block], sem.at[1, i]),
        ):
            copy.start()
            leaving.append(copy)
    for copy in leaving:
        copy.wait()


def call(kernel, operands, outs, scratch=()):
    return pl.pallas_call(
        kernel,
        out_shape=[jax.ShapeDtypeStruct(shape, kind) for shape, kind, _ in outs],
        in_specs=[spec for _, spec in operands],
        out_specs=[spec for _, _, spec in outs],
        scratch_shapes=list(scratch),
        compiler_params=pltpu.CompilerParams(vmem_limit_bytes=VMEM_LIMIT),
    )(*[array for array, _ in operands])


def fuse(function, *arrays):
    outs = jax.eval_shape(function, *arrays)

    def kernel(*refs):
        results = function(*[ref[...] for ref in refs[: len(arrays)]])
        for ref, result in zip(refs[len(arrays) :], results, strict=True):
            ref[...] = result

    return call(
        kernel,
        [(array, VMEM_SPEC) for array in arrays],
        [(out.shape, out.dtype, VMEM_SPEC) for out in outs],
    )


def scan_levels(axis, growth, gained):
    count = lax.axis_size(axis)
    kept = []
    size = 1
    while size < count:
        need_growth = 2 * size < count
        got_gained, got_growth = [], []
        for reach in range(1, size + 1):
            pairs = [
                (b + size - 1, b + size - 1 + reach)
                for b in range(0, count, 2 * size)
                if b + size - 1 + reach < count
            ]
            got_gained.append(lax.ppermute(gained, axis, pairs))
            if need_growth:
                later = [pair for pair in pairs if pair[0] >= 2 * size]
                got_growth.append(lax.ppermute(growth, axis, later))
        kept.append((got_gained, got_growth))
        if need_growth and 4 * size < count:

            def both(growth, gained, *got):
                new_gained, new_growth = sum(got[: len(got) // 2]), sum(got[len(got) // 2 :])
                return growth * new_growth, growth * new_gained + gained

            growth, gained = fuse(both, growth, gained, *got_gained, *got_growth)
        elif need_growth:
            (gained,) = fuse(
                lambda growth, gained, *got: (growth * sum(got) + gained,), growth, gained, *got_gained
            )
        size *= 2
    return kept


def finish_scan(axis, levels):
    place = lax.axis_index(axis)
    before_growth = before_gained = None
    for level, (got_gained, got_growth) in enumerate(levels):
        new_gained = sum(got_gained)
        upper = (place // 2**level) % 2 == 1
        if before_gained is None:
            before_gained = new_gained
        else:
            before_gained = before_growth * new_gained + before_gained
        if got_growth:
            new_growth = sum(got_growth)
            if before_growth is None:
                before_growth = jnp.where(upper, new_growth, 1.0)
            else:
                before_growth = jnp.where(upper, before_growth * new_growth, before_growth)
    return before_gained


def flatten(levels):
    leaves, tree = jax.tree.flatten(levels)
    return leaves, lambda values: jax.tree.unflatten(tree, values)


def local(packed, light_field, gas_density, phase_x, phase_y):
    width_x, width_y = phase_x.shape[0], phase_y.shape[0]
    radix_x, radix_y = width_x // LANES, width_y // LANES
    _, across, times, _ = light_field.shape
    group = ("zl", "core", "trans") if packed else ("core", "trans")
    later = "zh" if packed else ("zh", "zl")
    whole = ("zh", "zl")
    slabs = lax.axis_size(group)
    width = width_y // slabs
    slab = lax.axis_index(group)
    trans = lax.axis_size("trans")
    density_y = lax.dynamic_slice_in_dim(gas_density, slab * width, width, 1)
    density_x = lax.dynamic_slice_in_dim(gas_density, lax.axis_index("trans") * across, across, 0)
    if packed:
        density_y = jnp.concatenate([density_y] * times, axis=1)
        sent_shape = (slabs, 2, 1, across, times * width)
    else:
        sent_shape = (slabs, 2, times, across, width)
    inner, lanes = sent_shape[2], sent_shape[4]
    total = (slabs // trans) * inner
    rows = times * across

    def vmem(*shapes):
        return [(shape, F32, VMEM_SPEC) for shape in shapes]

    scratch_y = [
        pltpu.VMEM((radix_y, 3, rows, 2 * LANES), BF16),
        pltpu.VMEM((radix_y, rows, 2 * LANES), F32),
    ]
    scratch_x = [
        pltpu.VMEM((radix_x, 6 * LANES, total * lanes), BF16),
        pltpu.VMEM((radix_x, 2 * LANES, total * lanes), F32),
    ]
    table_y_shape = (radix_y, 3, 2, LANES, LANES)
    phase_y = phase_y.reshape(radix_y, LANES)
    (table_x,) = call(
        functools.partial(table_kernel, -1),
        [(phase_x.reshape(radix_x, LANES), VMEM_SPEC)],
        [((radix_x, 3, 2, LANES, LANES), BF16, VMEM_SPEC)],
    )
    (sent,) = call(
        functools.partial(first_kernel, packed),
        [(light_field, ANY_SPEC), (phase_y, ANY_SPEC)],
        [(sent_shape, F32, HBM_SPEC)],
        [pltpu.VMEM(table_y_shape, BF16)]
        + scratch_y
        + [
            pltpu.VMEM(light_field.shape, F32),
            pltpu.VMEM(phase_y.shape, F32),
            pltpu.VMEM(sent_shape, F32),
            pltpu.SemaphoreType.DMA((1 + across // min(16, across),)),
        ],
    )
    received = lax.all_to_all(sent, group, 0, 0, tiled=True)
    cells = (width_x, lanes)
    last = (width_x // 2, lanes) if packed else cells
    field, growth, gained, last_growth, last_gained = call(
        functools.partial(second_kernel, packed),
        [(received, VMEM_SPEC), (table_x, VMEM_SPEC), (density_y, VMEM_SPEC)],
        vmem((2, total) + cells, (total,) + cells, (total,) + cells, last, last),
        scratch_x,
    )
    levels = scan_levels(later, last_growth, last_gained)
    if len(levels) == 1 and len(levels[0][0]) == 1:
        entering = levels[0][0][0]
    else:
        leaves, rebuild = flatten(levels)
        (entering,) = fuse(lambda *got: (finish_scan(later, rebuild(got)),), *leaves)
    sent, token = call(
        functools.partial(third_kernel, packed),
        [(array, VMEM_SPEC) for array in (field, growth, gained, entering, table_x)],
        [(sent_shape, F32, HBM_SPEC), ((8, LANES), F32, VMEM_SPEC)],
        scratch_x + [pltpu.VMEM(sent_shape, F32), pltpu.SemaphoreType.DMA((slabs // trans,))],
    )
    received = lax.all_to_all(sent, group, 0, 0, tiled=True)
    (table_y,) = call(
        functools.partial(table_kernel, 1),
        [(phase_y, VMEM_SPEC), (token, VMEM_SPEC)],
        [(table_y_shape, BF16, VMEM_SPEC)],
    )
    cells = (across, width_y)
    half = (2, across // 2, width_y)
    field, growth, gained, mine, theirs = call(
        functools.partial(fourth_kernel, packed),
        [(received, VMEM_SPEC), (table_y, VMEM_SPEC), (density_x, VMEM_SPEC)],
        vmem((2, times) + cells, (times,) + cells, (times,) + cells, half, half),
        scratch_y,
    )
    swap = [(0, 1), (1, 0)]
    other = lax.ppermute(theirs, "core", swap)

    def ordered(mine, other):
        first = lax.axis_index("core") == 0
        early = [jnp.where(first, mine[i], other[i]) for i in range(2)]
        late = [jnp.where(first, other[i], mine[i]) for i in range(2)]
        return early, late

    def chip_map(mine, other):
        early, late = ordered(mine, other)
        return late[0] * early[0], late[0] * early[1] + late[1]

    levels = scan_levels(whole, *fuse(chip_map, mine, other))
    leaves, rebuild = flatten(levels)

    def hand_over(mine, other, *got):
        early, _ = ordered(mine, other)
        first = lax.axis_index("core") == 0
        entering = finish_scan(whole, rebuild(got))
        halfway = early[0] * entering + early[1]
        return jnp.where(first, entering, halfway), jnp.where(first, halfway, entering)

    kept, given = fuse(hand_over, mine, other, *leaves)
    given = lax.ppermute(given, "core", swap)
    chunks = across // min(16, across // 2)
    return call(
        fifth_kernel,
        [(array, VMEM_SPEC) for array in (field, growth, gained, kept, given)],
        [(light_field.shape, F32, HBM_SPEC), ((across, times, width_y), F32, HBM_SPEC)],
        [
            pltpu.VMEM(light_field.shape, F32),
            pltpu.VMEM((across, times, width_y), F32),
            pltpu.SemaphoreType.DMA((2, chunks)),
        ],
    )


def solution(mesh):
    slabs, trans = mesh.shape["tm"], mesh.shape["trans"]

    def run(light_field, gas_density, phase_x, phase_y):
        times = light_field.shape[2] // slabs
        width = phase_y.shape[0] // (trans * 4)
        packed = (
            slabs % 4 == 0
            and slabs > 4
            and times == 2
            and times * width == LANES
            and phase_x.shape[0] % (2 * LANES) == 0
        )
        pair = 2 if packed else 1
        split = Mesh(
            mesh.devices.reshape(slabs // (2 * pair), pair, 2, trans), ("zh", "zl", "core", "trans")
        )
        time_axes = ("zh", "zl", "core")
        placed = (P(None, "trans", time_axes, None), P(), P(), P())
        return jax.shard_map(
            functools.partial(local, packed),
            mesh=split,
            in_specs=placed,
            out_specs=(P(None, "trans", time_axes, None), P("trans", time_axes, None)),
            check_vma=False,
        )(light_field, gas_density, phase_x, phase_y)

    return run
```

```python
import functools
import math

import jax
import jax.numpy as jnp
from jax import lax
from jax.experimental import pallas as pl
from jax.experimental.pallas import tpu as pltpu
from jax.sharding import Mesh
from jax.sharding import PartitionSpec as P

PHOTONS = 8
STEPS = 2
RATE_COEF = 1.8e-08
RECOMB = 0.02
KERR_COEF = 0.3
PLASMA = 4.0
LANES = 128
HALF = LANES // 2
GROUP = {True: ("zl", "core", "trans"), False: ("core", "trans")}
LATER = {True: ("zh",), False: ("zh", "zl")}
VMEM_LIMIT = 16 * 1024 * 1024
F32 = jnp.float32
BF16 = jnp.bfloat16
VMEM_SPEC = pl.BlockSpec(memory_space=pltpu.VMEM)
ANY_SPEC = pl.BlockSpec(memory_space=pl.ANY)
HBM_SPEC = pl.BlockSpec(memory_space=pltpu.MemorySpace.HBM)


def sincos(quarter):
    turns = jnp.floor(quarter * (2.0 / math.pi) + 0.5)
    rest = quarter - turns * 1.5703125
    rest = rest - turns * 4.837512969970703125e-4
    rest = rest - turns * 7.54978995489188e-8
    square = rest * rest
    sine = ((-1.9515295891e-4 * square + 8.3321608736e-3) * square - 1.6666654611e-1) * square
    sine = sine * rest + rest
    cosine = (2.443315711809948e-5 * square - 1.388731625493765e-3) * square
    cosine = (cosine + 4.166664568298827e-2) * (square * square) - 0.5 * square + 1.0
    for _ in range(2):
        twice = sine + sine
        sine, cosine = twice * cosine, 1.0 - twice * sine
    return sine, cosine


def split3(value):
    high = value.astype(BF16)
    rest = value - high.astype(F32)
    middle = rest.astype(BF16)
    low = (rest - middle.astype(F32)).astype(BF16)
    return high, middle, low


def turned(value, order, position, sign):
    re, im = value
    eighth = (position * 8) // order
    if (position * 8) % order == 0 and eighth % 2 == 0:
        quarter = (eighth // 2 * sign) % 4
        return ((re, im), (-im, re), (-re, -im), (im, -re))[quarter]
    angle = sign * 2.0 * math.pi * position / order
    c, s = math.cos(angle), math.sin(angle)
    if (position * 8) % order == 0:
        root = math.sqrt(0.5)
        sc, ss = math.copysign(1, c), math.copysign(1, s)
        one = re - im if sc == ss else re + im
        two = re + im if sc == ss else re - im
        new_re = one * (root * sc)
        new_im = two * (root * ss) if sc == ss else two * (root * ss)
        return (new_re, new_im)
    return (re * c - im * s, re * s + im * c)


def small_dft(values, sign):
    count = len(values)
    if count == 1:
        return values
    even = small_dft(values[0::2], sign)
    odd = small_dft(values[1::2], sign)
    upper, lower = [], []
    for k in range(count // 2):
        other = turned(odd[k], count, k, sign)
        upper.append((even[k][0] + other[0], even[k][1] + other[1]))
        lower.append((even[k][0] - other[0], even[k][1] - other[1]))
    return upper + lower


def ionise(re, im, density):
    intensity = re * re + im * im
    power = intensity * intensity
    power = power * power
    rate = RATE_COEF * (power * power)
    loss = rate + RECOMB
    decay = jnp.exp(-loss)
    source = (1.0 - decay) * density * rate / loss
    return decay, source


def rotate(re, im, electrons):
    intensity = re * re + im * im
    sine, cosine = sincos((0.25 * KERR_COEF) * intensity - (0.25 * PLASMA) * electrons)
    return re * cosine - im * sine, re * sine + im * cosine


def wave(shape, order, sign):
    product = lax.broadcasted_iota(jnp.int32, shape, 0) * lax.broadcasted_iota(jnp.int32, shape, 1)
    sine, cosine = sincos((product % order).astype(F32) * (0.5 * math.pi / order))
    return cosine, sign * sine


def toeplitz_blocks(phase, radix, sign):
    length = radix * LANES
    waves = jnp.concatenate(wave((LANES, LANES), length, sign), axis=1)
    block_re, block_im = wave((radix, LANES), radix, sign)
    block_re, block_im = block_re * (1.0 / length), block_im * (1.0 / length)
    sine, cosine = sincos(0.25 * phase)
    lane = lax.broadcasted_iota(jnp.int32, phase.shape, 1) % radix
    picked = [jnp.where(lane == k, part, 0.0) for part in (cosine, sine) for k in range(radix)]
    spectrum = jnp.dot(
        jnp.concatenate(picked, axis=0),
        waves,
        precision=lax.Precision.HIGHEST,
        preferred_element_type=F32,
    )
    half = radix * radix
    row = lax.broadcasted_iota(jnp.int32, (LANES, LANES), 0)
    column = lax.broadcasted_iota(jnp.int32, (LANES, LANES), 1)
    direct = column >= row
    blocks = []
    for k in range(radix):
        ours = slice(k * radix, (k + 1) * radix)
        theirs = slice(half + k * radix, half + (k + 1) * radix)
        re = spectrum[ours, :LANES] - spectrum[theirs, LANES:]
        im = spectrum[ours, LANES:] + spectrum[theirs, :LANES]
        full_re = jnp.sum(re * block_re - im * block_im, axis=0, keepdims=True)
        full_im = jnp.sum(re * block_im + im * block_re, axis=0, keepdims=True)
        spread_re = jnp.broadcast_to(full_re, (LANES, LANES))
        spread_im = jnp.broadcast_to(full_im, (LANES, LANES))
        rolled = (
            pltpu.roll(spread_re, 0, 1, stride=1, stride_axis=0),
            pltpu.roll(spread_im, 0, 1, stride=1, stride_axis=0),
        )
        wrapped = turned(rolled, radix, k, -sign)
        blocks.append(
            (jnp.where(direct, rolled[0], wrapped[0]), jnp.where(direct, rolled[1], wrapped[1]))
        )
    return blocks


def store_parts(table_ref, blocks):
    for k, (re, im) in enumerate(blocks):
        for part, (a, b) in enumerate(zip(split3(re), split3(im), strict=True)):
            table_ref[k, part, 0] = a
            table_ref[k, part, 1] = b


def table_kernel(sign, phase_ref, *refs):
    table_ref = refs[-1]
    store_parts(table_ref, toeplitz_blocks(phase_ref[...], table_ref.shape[0], sign))


def forward_y(load, start, step, radix, parts_ref):
    blocks = small_dft([load(a) for a in range(radix)], -1)
    for k, (re, im) in enumerate(blocks):
        for part, (a, b) in enumerate(zip(split3(re), split3(im), strict=True)):
            parts_ref[k, part, start : start + step, :LANES] = a
            parts_ref[k, part, start : start + step, LANES:] = b


def product_y(parts_ref, table_ref, out_ref, radix):
    for k in range(radix):
        high, middle, low = parts_ref[k, 0], parts_ref[k, 1], parts_ref[k, 2]
        left = jnp.concatenate([high, high, high, middle, middle, low], axis=1)
        rights = []
        for part in range(3):
            re, im = table_ref[k, part, 0], table_ref[k, part, 1]
            rights.append(jnp.concatenate([re, im], axis=1))
            rights.append(jnp.concatenate([-im, re], axis=1))
        right = jnp.concatenate(rights + rights[:4] + rights[:2], axis=0)
        out_ref[k] = jnp.dot(left, right, preferred_element_type=F32)


def backward_y(out_ref, start, step, radix):
    picked = [
        (out_ref[k, start : start + step, :LANES], out_ref[k, start : start + step, LANES:])
        for k in range(radix)
    ]
    return small_dft(picked, 1)


def upper_lanes(shape):
    return lax.broadcasted_iota(jnp.int32, shape, 1) >= HALF


def swap_halves(value):
    return pltpu.roll(value, HALF, 1)


def first_kernel(
    packed, light_hbm, phase_hbm, send_hbm, table_ref, parts_ref, mid_ref, light_ref, rows_ref, phase_ref,
    send_ref, sem,
):
    radix = table_ref.shape[0]
    _, across, times, _ = light_ref.shape
    width = send_ref.shape[-1]
    step = min(16, across)
    chunks = range(0, across, step)
    phase_copy = pltpu.make_async_copy(phase_hbm, phase_ref, sem.at[0])
    phase_copy.start()
    arriving = []
    for i, x in enumerate(chunks):
        rows = pl.ds(x, step)
        copy = pltpu.make_async_copy(light_hbm.at[:, rows], light_ref.at[:, rows], sem.at[1 + i])
        copy.start()
        arriving.append(copy)
    phase_copy.wait()
    store_parts(table_ref, toeplitz_blocks(phase_ref[...], radix, 1))
    for copy, x in zip(arriving, chunks, strict=True):
        copy.wait()
        for t in range(times):

            for c in range(2):
                for start in range(x, x + step, 8):
                    rows_ref[c, t, start : start + 8, :] = light_ref[c, start : start + 8, t, :]

            def load(a, x=x, t=t):
                lanes = slice(a * LANES, (a + 1) * LANES)
                rows = slice(x, x + step)
                return rows_ref[0, t, rows, lanes], rows_ref[1, t, rows, lanes]

            forward_y(load, t * across + x, step, radix, parts_ref)
    product_y(parts_ref, table_ref, mid_ref, radix)
    leaving = []
    upper = upper_lanes((8, LANES))
    for i, begin in enumerate(chunks):
        for x in range(begin, begin + step, 8):
            rows = slice(x, x + 8)
            results = [backward_y(mid_ref, t * across + x, 8, radix) for t in range(times)]
            for a in range(radix):
                for c in range(2):
                    values = [results[t][a][c] for t in range(times)]
                    if packed:
                        one, two = values
                        send_ref[2 * a, c, 0, rows, :] = jnp.where(upper, swap_halves(two), one)
                        send_ref[2 * a + 1, c, 0, rows, :] = jnp.where(upper, two, swap_halves(one))
                    elif width >= LANES:
                        slab, offset = a * LANES // width, a * LANES % width
                        for t in range(times):
                            send_ref[slab, c, t, rows, offset : offset + LANES] = values[t]
                    else:
                        for t in range(times):
                            for piece in range(LANES // width):
                                slab = a * LANES // width + piece
                                lanes = slice(piece * width, (piece + 1) * width)
                                send_ref[slab, c, t, rows, :] = values[t][:, lanes]
        rows = pl.ds(begin, step)
        copy = pltpu.make_async_copy(
            send_ref.at[:, :, :, rows], send_hbm.at[:, :, :, rows], sem.at[1 + i]
        )
        copy.start()
        leaving.append(copy)
    for copy in leaving:
        copy.wait()


def put_x(parts_ref, lanes, start, values):
    step = values[0][0].shape[0]
    for k, (re, im) in enumerate(small_dft(values, -1)):
        for part, (a, b) in enumerate(zip(split3(re), split3(im), strict=True)):
            base = part * 2 * LANES
            parts_ref[k, base + start : base + start + step, lanes] = a
            parts_ref[k, base + LANES + start : base + LANES + start + step, lanes] = b


def product_x(parts_ref, table_ref, out_ref, radix):
    for k in range(radix):
        lefts = []
        for part in range(3):
            re, im = table_ref[k, part, 0], table_ref[k, part, 1]
            lefts.append(jnp.concatenate([re, im], axis=0))
            lefts.append(jnp.concatenate([-im, re], axis=0))
        left = jnp.concatenate(lefts + lefts[:4] + lefts[:2], axis=1)
        high = parts_ref[k, : 2 * LANES]
        middle = parts_ref[k, 2 * LANES : 4 * LANES]
        low = parts_ref[k, 4 * LANES :]
        right = jnp.concatenate([high, high, high, middle, middle, low], axis=0)
        out_ref[k] = jnp.dot(left, right, preferred_element_type=F32)


def get_x(out_ref, lanes, start, step, radix):
    picked = [
        (out_ref[k, start : start + step, lanes], out_ref[k, LANES + start : LANES + start + step, lanes])
        for k in range(radix)
    ]
    return small_dft(picked, 1)


def second_kernel(
    packed, recv_ref, table_ref, density_ref, field_ref, growth_ref, gained_ref, last_growth_ref, last_gained_ref,
    parts_ref, mid_ref,
):
    radix = table_ref.shape[0]
    sources, _, times, across, width = recv_ref.shape
    trans = (radix * LANES) // across
    step = min(16, across)
    total = (sources // trans) * times

    def at(c, t, x):
        place, inner = t // times, t % times
        return recv_ref[place * trans + x // across, c, inner, x % across : x % across + step, :]

    for t in range(total):
        lanes = slice(t * width, (t + 1) * width)
        for start in range(0, LANES, step):
            values = [
                (at(0, t, a * LANES + start), at(1, t, a * LANES + start)) for a in range(radix)
            ]
            put_x(parts_ref, lanes, start, values)
    product_x(parts_ref, table_ref, mid_ref, radix)
    upper = upper_lanes((8, LANES))
    for start in range(0, LANES, 8):
        carry = [None] * radix
        for t in range(total):
            lanes = slice(t * width, (t + 1) * width)
            for a, (re, im) in enumerate(get_x(mid_ref, lanes, start, 8, radix)):
                rows = slice(a * LANES + start, a * LANES + start + 8)
                field_ref[0, t, rows, :] = re
                field_ref[1, t, rows, :] = im
                growth, gained = ionise(re, im, density_ref[rows, :])
                if packed:
                    gained = jnp.where(upper, growth * swap_halves(gained) + gained, gained)
                    growth = jnp.where(upper, growth * swap_halves(growth), growth)
                if carry[a] is not None:
                    gained = growth * carry[a][1] + gained
                    growth = growth * carry[a][0]
                growth_ref[t, rows, :] = growth
                gained_ref[t, rows, :] = gained
                if packed:
                    growth = jnp.where(upper, growth, swap_halves(growth))
                    gained = jnp.where(upper, gained, swap_halves(gained))
                carry[a] = (growth, gained)
        for a in range(radix // 2 if packed else radix):
            rows = slice(a * LANES + start, a * LANES + start + 8)
            growth, gained = carry[a]
            if packed:
                growth = jnp.where(upper, carry[a + radix // 2][0], growth)
                gained = jnp.where(upper, carry[a + radix // 2][1], gained)
            last_growth_ref[rows, :] = growth
            last_gained_ref[rows, :] = gained


def third_kernel(packed, rebuild, leaves, field_ref, growth_ref, gained_ref, table_ref, *refs):
    got_refs = refs[:leaves]
    send_hbm, token_ref, parts_ref, mid_ref, send_ref, sem = refs[leaves:]

    def enter(start, step):
        got = [ref[start : start + step, :] for ref in got_refs]
        return finish_scan(LATER[packed], rebuild(got))

    radix = table_ref.shape[0]
    _, total, _, width = field_ref.shape
    slabs, _, times, across, _ = send_ref.shape
    trans = (radix * LANES) // across
    token_ref[...] = jnp.zeros_like(token_ref)
    step = 16
    upper = upper_lanes((step, LANES))
    for start in range(0, LANES, step):
        entering = []
        for a in range(radix):
            if packed:
                base = (a % (radix // 2)) * LANES + start
                value = enter(base, step)
                other = swap_halves(value)
                first = a < radix // 2
                entering.append(jnp.where(upper, other if first else value, value if first else other))
            else:
                entering.append(enter(a * LANES + start, step))
        for t in range(total):
            lanes = slice(t * width, (t + 1) * width)
            values = []
            for a in range(radix):
                rows = slice(a * LANES + start, a * LANES + start + step)
                electrons = growth_ref[t, rows, :] * entering[a] + gained_ref[t, rows, :]
                values.append(rotate(field_ref[0, t, rows, :], field_ref[1, t, rows, :], electrons))
            put_x(parts_ref, lanes, start, values)
    product_x(parts_ref, table_ref, mid_ref, radix)
    leaving = []
    for t in range(total):
        lanes = slice(t * width, (t + 1) * width)
        place, inner = t // times, t % times
        for start in range(0, LANES, 8):
            for a, pair in enumerate(get_x(mid_ref, lanes, start, 8, radix)):
                x = a * LANES + start
                row = x % across
                for c in range(2):
                    send_ref[place * trans + x // across, c, inner, row : row + 8, :] = pair[c]
        if inner == times - 1:
            block = pl.ds(place * trans, trans)
            copy = pltpu.make_async_copy(send_ref.at[block], send_hbm.at[block], sem.at[place])
            copy.start()
            leaving.append(copy)
    for copy in leaving:
        copy.wait()


def fourth_kernel(
    packed, recv_ref, table_ref, density_ref, field_ref, growth_ref, gained_ref, mine_ref, theirs_ref,
    parts_ref, mid_ref,
):
    radix = table_ref.shape[0]
    _, times, across, _ = field_ref.shape
    width = recv_ref.shape[-1]
    core = lax.axis_index("core")
    step = min(16, across)
    upper = upper_lanes((step, LANES))

    def part(c, t, x, a):
        rows = slice(x, x + step)
        if packed:
            one, two = recv_ref[2 * a, c, 0, rows, :], recv_ref[2 * a + 1, c, 0, rows, :]
            if t == 0:
                return jnp.where(upper, swap_halves(two), one)
            return jnp.where(upper, two, swap_halves(one))
        if width >= LANES:
            slab, offset = a * LANES // width, a * LANES % width
            return recv_ref[slab, c, t, rows, offset : offset + LANES]
        pieces = LANES // width
        return jnp.concatenate(
            [recv_ref[a * pieces + p, c, t, rows, :] for p in range(pieces)], axis=1
        )

    for x in range(0, across, step):
        for t in range(times):

            def load(a, x=x, t=t):
                return part(0, t, x, a), part(1, t, x, a)

            forward_y(load, t * across + x, step, radix, parts_ref)
    product_y(parts_ref, table_ref, mid_ref, radix)
    half = across // 2
    for x in range(0, across, 8):
        rows = slice(x, x + 8)
        growth, gained = [None] * radix, [None] * radix
        for t in range(times):
            for a, (re, im) in enumerate(backward_y(mid_ref, t * across + x, 8, radix)):
                lanes = slice(a * LANES, (a + 1) * LANES)
                field_ref[0, t, rows, lanes] = re
                field_ref[1, t, rows, lanes] = im
                decay, source = ionise(re, im, density_ref[rows, lanes])
                if t == 0:
                    growth[a], gained[a] = decay, source
                else:
                    gained[a] = decay * gained[a] + source
                    growth[a] = growth[a] * decay
                growth_ref[t, rows, lanes] = growth[a]
                gained_ref[t, rows, lanes] = gained[a]
    last = times - 1

    def hand_out(own):
        kept, given = slice(own * half, (own + 1) * half), slice((1 - own) * half, (2 - own) * half)
        mine_ref[0] = growth_ref[last, kept, :]
        mine_ref[1] = gained_ref[last, kept, :]
        theirs_ref[0] = growth_ref[last, given, :]
        theirs_ref[1] = gained_ref[last, given, :]

    pl.when(core == 0)(functools.partial(hand_out, 0))
    pl.when(core == 1)(functools.partial(hand_out, 1))


def fifth_kernel(
    field_ref, growth_ref, gained_ref, kept_ref, given_ref, light_hbm, electrons_hbm, light_ref, electrons_ref, sem
):
    _, times, across, length = field_ref.shape
    half = across // 2
    core = lax.axis_index("core")
    step = min(16, half)
    leaving = []
    for i, begin in enumerate(range(0, across, step)):
        for x in range(begin, begin + step, 8):
            own, row = x // half, x % half
            rows = slice(x, x + 8)
            entering = jnp.where(core == own, kept_ref[row : row + 8, :], given_ref[row : row + 8, :])
            for t in range(times):
                results = []
                for a in range(length // LANES):
                    lanes = slice(a * LANES, (a + 1) * LANES)
                    electrons = (
                        growth_ref[t, rows, lanes] * entering[:, lanes] + gained_ref[t, rows, lanes]
                    )
                    re, im = rotate(field_ref[0, t, rows, lanes], field_ref[1, t, rows, lanes], electrons)
                    results.append((re, im, electrons))
                re, im, electrons = (jnp.concatenate(part, axis=1) for part in zip(*results, strict=True))
                light_ref[0, rows, t, :] = re
                light_ref[1, rows, t, :] = im
                electrons_ref[rows, t, :] = electrons
        block = pl.ds(begin, step)
        for copy in (
            pltpu.make_async_copy(light_ref.at[:, block], light_hbm.at[:, block], sem.at[0, i]),
            pltpu.make_async_copy(electrons_ref.at[block], electrons_hbm.at[block], sem.at[1, i]),
        ):
            copy.start()
            leaving.append(copy)
    for copy in leaving:
        copy.wait()


def call(kernel, operands, outs, scratch=()):
    return pl.pallas_call(
        kernel,
        out_shape=[jax.ShapeDtypeStruct(shape, kind) for shape, kind, _ in outs],
        in_specs=[spec for _, spec in operands],
        out_specs=[spec for _, _, spec in outs],
        scratch_shapes=list(scratch),
        compiler_params=pltpu.CompilerParams(vmem_limit_bytes=VMEM_LIMIT),
    )(*[array for array, _ in operands])


def in_hbm(array):
    return pltpu.with_memory_space_constraint(array, pltpu.MemorySpace.HBM)


def fuse(function, *arrays):
    outs = jax.eval_shape(function, *arrays)

    def kernel(*refs):
        results = function(*[ref[...] for ref in refs[: len(arrays)]])
        for ref, result in zip(refs[len(arrays) :], results, strict=True):
            ref[...] = result

    return call(
        kernel,
        [(array, VMEM_SPEC) for array in arrays],
        [(out.shape, out.dtype, VMEM_SPEC) for out in outs],
    )


def both_ways(pairs):
    return pairs + [(b, a) for a, b in pairs]


def scan_levels(axis, growth, gained):
    count = lax.axis_size(axis)
    kept = []
    size = 1
    while size < count:
        need_growth = 2 * size < count
        got_gained, got_growth = [], []
        for reach in range(1, size + 1):
            pairs = [
                (b + size - 1, b + size - 1 + reach)
                for b in range(0, count, 2 * size)
                if b + size - 1 + reach < count
            ]
            got_gained.append(lax.ppermute(gained, axis, both_ways(pairs)))
            if need_growth:
                later = [pair for pair in pairs if pair[0] >= 2 * size]
                got_growth.append(lax.ppermute(growth, axis, both_ways(later)))
        kept.append((got_gained, got_growth))
        if need_growth and 4 * size < count:

            def both(growth, gained, *got):
                new_gained, new_growth = sum(got[: len(got) // 2]), sum(got[len(got) // 2 :])
                return growth * new_growth, growth * new_gained + gained

            growth, gained = fuse(both, growth, gained, *got_gained, *got_growth)
        elif need_growth:
            (gained,) = fuse(
                lambda growth, gained, *got: (growth * sum(got) + gained,), growth, gained, *got_gained
            )
        size *= 2
    return kept


def finish_scan(axis, levels):
    place = lax.axis_index(axis)
    before_growth = before_gained = None
    for level, (got_gained, got_growth) in enumerate(levels):
        new_gained = sum(got_gained)
        upper = (place // 2**level) % 2 == 1
        if before_gained is None:
            before_gained = jnp.where(upper, new_gained, 0.0)
        else:
            new_gained = before_growth * new_gained + before_gained
            before_gained = jnp.where(upper, new_gained, before_gained)
        if got_growth:
            new_growth = sum(got_growth)
            if before_growth is None:
                before_growth = jnp.where(upper, new_growth, 1.0)
            else:
                before_growth = jnp.where(upper, before_growth * new_growth, before_growth)
    return before_gained


def flatten(levels):
    leaves, tree = jax.tree.flatten(levels)
    return leaves, lambda values: jax.tree.unflatten(tree, values)


def local(packed, light_field, gas_density, phase_x, phase_y):
    width_x, width_y = phase_x.shape[0], phase_y.shape[0]
    radix_x, radix_y = width_x // LANES, width_y // LANES
    _, across, times, _ = light_field.shape
    group = GROUP[packed]
    later = LATER[packed]
    whole = ("zh", "zl")
    slabs = lax.axis_size(group)
    width = width_y // slabs
    slab = lax.axis_index(group)
    trans = lax.axis_size("trans")
    density_y = lax.dynamic_slice_in_dim(gas_density, slab * width, width, 1)
    density_x = lax.dynamic_slice_in_dim(gas_density, lax.axis_index("trans") * across, across, 0)
    density_y, density_x = lax.optimization_barrier((density_y, density_x))
    if packed:
        density_y = jnp.concatenate([density_y] * times, axis=1)
        sent_shape = (slabs, 2, 1, across, times * width)
    else:
        sent_shape = (slabs, 2, times, across, width)
    inner, lanes = sent_shape[2], sent_shape[4]
    total = (slabs // trans) * inner
    rows = times * across

    def vmem(*shapes):
        return [(shape, F32, VMEM_SPEC) for shape in shapes]

    scratch_y = [
        pltpu.VMEM((radix_y, 3, rows, 2 * LANES), BF16),
        pltpu.VMEM((radix_y, rows, 2 * LANES), F32),
    ]
    scratch_x = [
        pltpu.VMEM((radix_x, 6 * LANES, total * lanes), BF16),
        pltpu.VMEM((radix_x, 2 * LANES, total * lanes), F32),
    ]
    table_y_shape = (radix_y, 3, 2, LANES, LANES)
    phase_y = phase_y.reshape(radix_y, LANES)
    (table_x,) = call(
        functools.partial(table_kernel, -1),
        [(phase_x.reshape(radix_x, LANES), VMEM_SPEC)],
        [((radix_x, 3, 2, LANES, LANES), BF16, VMEM_SPEC)],
    )
    (sent,) = call(
        functools.partial(first_kernel, packed),
        [(in_hbm(light_field), HBM_SPEC), (in_hbm(phase_y), HBM_SPEC)],
        [(sent_shape, F32, HBM_SPEC)],
        [pltpu.VMEM(table_y_shape, BF16)]
        + scratch_y
        + [
            pltpu.VMEM(light_field.shape, F32),
            pltpu.VMEM((2, times, across, width_y), F32),
            pltpu.VMEM(phase_y.shape, F32),
            pltpu.VMEM(sent_shape, F32),
            pltpu.SemaphoreType.DMA((1 + across // min(16, across),)),
        ],
    )
    received = lax.all_to_all(sent, group, 0, 0, tiled=True)
    cells = (width_x, lanes)
    last = (width_x // 2, lanes) if packed else cells
    field, growth, gained, last_growth, last_gained = call(
        functools.partial(second_kernel, packed),
        [(received, VMEM_SPEC), (table_x, VMEM_SPEC), (density_y, VMEM_SPEC)],
        vmem((2, total) + cells, (total,) + cells, (total,) + cells, last, last),
        scratch_x,
    )
    levels = scan_levels(later, last_growth, last_gained)
    leaves, rebuild = flatten(levels)
    sent, token = call(
        functools.partial(third_kernel, packed, rebuild, len(leaves)),
        [(array, VMEM_SPEC) for array in (field, growth, gained, table_x, *leaves)],
        [(sent_shape, F32, HBM_SPEC), ((8, LANES), F32, VMEM_SPEC)],
        scratch_x + [pltpu.VMEM(sent_shape, F32), pltpu.SemaphoreType.DMA((slabs // trans,))],
    )
    received = lax.all_to_all(sent, group, 0, 0, tiled=True)
    (table_y,) = call(
        functools.partial(table_kernel, 1),
        [(phase_y, VMEM_SPEC), (token, VMEM_SPEC)],
        [(table_y_shape, BF16, VMEM_SPEC)],
    )
    cells = (across, width_y)
    half = (2, across // 2, width_y)
    field, growth, gained, mine, theirs = call(
        functools.partial(fourth_kernel, packed),
        [(received, VMEM_SPEC), (table_y, VMEM_SPEC), (density_x, VMEM_SPEC)],
        vmem((2, times) + cells, (times,) + cells, (times,) + cells, half, half),
        scratch_y,
    )
    swap = [(0, 1), (1, 0)]
    other = lax.ppermute(theirs, "core", swap)

    def ordered(mine, other):
        first = lax.axis_index("core") == 0
        early = [jnp.where(first, mine[i], other[i]) for i in range(2)]
        late = [jnp.where(first, other[i], mine[i]) for i in range(2)]
        return early, late

    def chip_map(mine, other):
        early, late = ordered(mine, other)
        return late[0] * early[0], late[0] * early[1] + late[1]

    levels = scan_levels(whole, *fuse(chip_map, mine, other))
    leaves, rebuild = flatten(levels)

    def hand_over(mine, other, *got):
        early, _ = ordered(mine, other)
        first = lax.axis_index("core") == 0
        entering = finish_scan(whole, rebuild(got))
        halfway = early[0] * entering + early[1]
        return jnp.where(first, entering, halfway), jnp.where(first, halfway, entering)

    kept, given = fuse(hand_over, mine, other, *leaves)
    given = lax.ppermute(given, "core", swap)
    chunks = across // min(16, across // 2)
    return call(
        fifth_kernel,
        [(array, VMEM_SPEC) for array in (field, growth, gained, kept, given)],
        [(light_field.shape, F32, HBM_SPEC), ((across, times, width_y), F32, HBM_SPEC)],
        [
            pltpu.VMEM(light_field.shape, F32),
            pltpu.VMEM((across, times, width_y), F32),
            pltpu.SemaphoreType.DMA((2, chunks)),
        ],
    )


def solution(mesh):
    slabs, trans = mesh.shape["tm"], mesh.shape["trans"]

    def run(light_field, gas_density, phase_x, phase_y):
        times = light_field.shape[2] // slabs
        width = phase_y.shape[0] // (trans * 4)
        packed = (
            slabs % 4 == 0
            and slabs > 4
            and times == 2
            and times * width == LANES
            and phase_x.shape[0] % (2 * LANES) == 0
        )
        pair = 2 if packed else 1
        split = Mesh(
            mesh.devices.reshape(slabs // (2 * pair), pair, 2, trans), ("zh", "zl", "core", "trans")
        )
        time_axes = ("zh", "zl", "core")
        placed = (P(None, "trans", time_axes, None), P(), P(), P())
        return jax.shard_map(
            functools.partial(local, packed),
            mesh=split,
            in_specs=placed,
            out_specs=(P(None, "trans", time_axes, None), P("trans", time_axes, None)),
            check_vma=False,
        )(light_field, gas_density, phase_x, phase_y)

    return run
```

```python
import functools
import math

import jax
import jax.numpy as jnp
from jax import lax
from jax.experimental import pallas as pl
from jax.experimental.pallas import tpu as pltpu
from jax.sharding import Mesh
from jax.sharding import PartitionSpec as P

PHOTONS = 8
STEPS = 2
RATE_COEF = 1.8e-08
RECOMB = 0.02
KERR_COEF = 0.3
PLASMA = 4.0
LANES = 128
HALF = LANES // 2
Z_AXES = ("zh", "zl")
GROUP = {True: ("zl", "core", "trans"), False: ("core", "trans")}
VMEM_LIMIT = 16 * 1024 * 1024
F32 = jnp.float32
BF16 = jnp.bfloat16
VMEM_SPEC = pl.BlockSpec(memory_space=pltpu.VMEM)
ANY_SPEC = pl.BlockSpec(memory_space=pl.ANY)
HBM_SPEC = pl.BlockSpec(memory_space=pltpu.MemorySpace.HBM)


def sincos(quarter):
    turns = jnp.floor(quarter * (2.0 / math.pi) + 0.5)
    rest = quarter - turns * 1.5703125
    rest = rest - turns * 4.837512969970703125e-4
    rest = rest - turns * 7.54978995489188e-8
    square = rest * rest
    sine = ((-1.9515295891e-4 * square + 8.3321608736e-3) * square - 1.6666654611e-1) * square
    sine = sine * rest + rest
    cosine = (2.443315711809948e-5 * square - 1.388731625493765e-3) * square
    cosine = (cosine + 4.166664568298827e-2) * (square * square) - 0.5 * square + 1.0
    for _ in range(2):
        twice = sine + sine
        sine, cosine = twice * cosine, 1.0 - twice * sine
    return sine, cosine


def split3(value):
    high = value.astype(BF16)
    rest = value - high.astype(F32)
    middle = rest.astype(BF16)
    low = (rest - middle.astype(F32)).astype(BF16)
    return high, middle, low


def turned(value, order, position, sign):
    re, im = value
    eighth = (position * 8) // order
    if (position * 8) % order == 0 and eighth % 2 == 0:
        quarter = (eighth // 2 * sign) % 4
        return ((re, im), (-im, re), (-re, -im), (im, -re))[quarter]
    angle = sign * 2.0 * math.pi * position / order
    c, s = math.cos(angle), math.sin(angle)
    if (position * 8) % order == 0:
        root = math.sqrt(0.5)
        sc, ss = math.copysign(1, c), math.copysign(1, s)
        one = re - im if sc == ss else re + im
        two = re + im if sc == ss else re - im
        new_re = one * (root * sc)
        new_im = two * (root * ss) if sc == ss else two * (root * ss)
        return (new_re, new_im)
    return (re * c - im * s, re * s + im * c)


def small_dft(values, sign):
    count = len(values)
    if count == 1:
        return values
    even = small_dft(values[0::2], sign)
    odd = small_dft(values[1::2], sign)
    upper, lower = [], []
    for k in range(count // 2):
        other = turned(odd[k], count, k, sign)
        upper.append((even[k][0] + other[0], even[k][1] + other[1]))
        lower.append((even[k][0] - other[0], even[k][1] - other[1]))
    return upper + lower


def ionise(re, im, density):
    intensity = re * re + im * im
    power = intensity * intensity
    power = power * power
    rate = RATE_COEF * (power * power)
    loss = rate + RECOMB
    decay = jnp.exp(-loss)
    source = (1.0 - decay) * density * rate / loss
    return decay, source


def rotate(re, im, electrons):
    intensity = re * re + im * im
    sine, cosine = sincos((0.25 * KERR_COEF) * intensity - (0.25 * PLASMA) * electrons)
    return re * cosine - im * sine, re * sine + im * cosine


def wave(shape, order, sign):
    product = lax.broadcasted_iota(jnp.int32, shape, 0) * lax.broadcasted_iota(jnp.int32, shape, 1)
    sine, cosine = sincos((product % order).astype(F32) * (0.5 * math.pi / order))
    return cosine, sign * sine


def toeplitz_blocks(phase, radix, sign):
    length = radix * LANES
    waves = jnp.concatenate(wave((LANES, LANES), length, sign), axis=1)
    block_re, block_im = wave((radix, LANES), radix, sign)
    block_re, block_im = block_re * (1.0 / length), block_im * (1.0 / length)
    sine, cosine = sincos(0.25 * phase)
    lane = lax.broadcasted_iota(jnp.int32, phase.shape, 1) % radix
    picked = [jnp.where(lane == k, part, 0.0) for part in (cosine, sine) for k in range(radix)]
    spectrum = jnp.dot(
        jnp.concatenate(picked, axis=0),
        waves,
        precision=lax.Precision.HIGHEST,
        preferred_element_type=F32,
    )
    half = radix * radix
    row = lax.broadcasted_iota(jnp.int32, (LANES, LANES), 0)
    column = lax.broadcasted_iota(jnp.int32, (LANES, LANES), 1)
    direct = column >= row
    blocks = []
    for k in range(radix):
        ours = slice(k * radix, (k + 1) * radix)
        theirs = slice(half + k * radix, half + (k + 1) * radix)
        re = spectrum[ours, :LANES] - spectrum[theirs, LANES:]
        im = spectrum[ours, LANES:] + spectrum[theirs, :LANES]
        full_re = jnp.sum(re * block_re - im * block_im, axis=0, keepdims=True)
        full_im = jnp.sum(re * block_im + im * block_re, axis=0, keepdims=True)
        spread_re = jnp.broadcast_to(full_re, (LANES, LANES))
        spread_im = jnp.broadcast_to(full_im, (LANES, LANES))
        rolled = (
            pltpu.roll(spread_re, 0, 1, stride=1, stride_axis=0),
            pltpu.roll(spread_im, 0, 1, stride=1, stride_axis=0),
        )
        wrapped = turned(rolled, radix, k, -sign)
        blocks.append(
            (jnp.where(direct, rolled[0], wrapped[0]), jnp.where(direct, rolled[1], wrapped[1]))
        )
    return blocks


def store_parts(table_ref, blocks):
    for k, (re, im) in enumerate(blocks):
        for part, (a, b) in enumerate(zip(split3(re), split3(im), strict=True)):
            table_ref[k, part, 0] = a
            table_ref[k, part, 1] = b


def table_kernel(sign, phase_ref, *refs):
    table_ref = refs[-1]
    store_parts(table_ref, toeplitz_blocks(phase_ref[...], table_ref.shape[0], sign))


def forward_y(load, start, step, radix, parts_ref):
    blocks = small_dft([load(a) for a in range(radix)], -1)
    for k, (re, im) in enumerate(blocks):
        for part, (a, b) in enumerate(zip(split3(re), split3(im), strict=True)):
            parts_ref[k, part, start : start + step, :LANES] = a
            parts_ref[k, part, start : start + step, LANES:] = b


def product_y(parts_ref, table_ref, out_ref, radix):
    for k in range(radix):
        high, middle, low = parts_ref[k, 0], parts_ref[k, 1], parts_ref[k, 2]
        left = jnp.concatenate([high, high, high, middle, middle, low], axis=1)
        rights = []
        for part in range(3):
            re, im = table_ref[k, part, 0], table_ref[k, part, 1]
            rights.append(jnp.concatenate([re, im], axis=1))
            rights.append(jnp.concatenate([-im, re], axis=1))
        right = jnp.concatenate(rights + rights[:4] + rights[:2], axis=0)
        out_ref[k] = jnp.dot(left, right, preferred_element_type=F32)


def backward_y(out_ref, start, step, radix):
    picked = [
        (out_ref[k, start : start + step, :LANES], out_ref[k, start : start + step, LANES:])
        for k in range(radix)
    ]
    return small_dft(picked, 1)


def upper_lanes(shape):
    return lax.broadcasted_iota(jnp.int32, shape, 1) >= HALF


def swap_halves(value):
    return pltpu.roll(value, HALF, 1)


def first_kernel(
    packed, light_hbm, phase_hbm, send_hbm, table_ref, parts_ref, mid_ref, light_ref, rows_ref, phase_ref,
    send_ref, sem,
):
    radix = table_ref.shape[0]
    _, across, times, _ = light_ref.shape
    width = send_ref.shape[-1]
    step = min(16, across)
    chunks = range(0, across, step)
    count = send_ref.shape[0] // 2
    flip = lax.rem(lax.axis_index("zh"), 2) if packed else 0
    phase_copy = pltpu.make_async_copy(phase_hbm, phase_ref, sem.at[0, 0])
    phase_copy.start()
    arriving = []
    for i, x in enumerate(chunks):
        rows = pl.ds(x, step)
        copy = pltpu.make_async_copy(light_hbm.at[:, rows], light_ref.at[:, rows], sem.at[1 + i, 0])
        copy.start()
        arriving.append(copy)
    phase_copy.wait()
    store_parts(table_ref, toeplitz_blocks(phase_ref[...], radix, 1))
    for copy, x in zip(arriving, chunks, strict=True):
        copy.wait()
        for t in range(times):

            for c in range(2):
                for start in range(x, x + step, 8):
                    rows_ref[c, t, start : start + 8, :] = light_ref[c, start : start + 8, t, :]

            def load(a, x=x, t=t):
                lanes = slice(a * LANES, (a + 1) * LANES)
                rows = slice(x, x + step)
                return rows_ref[0, t, rows, lanes], rows_ref[1, t, rows, lanes]

            forward_y(load, t * across + x, step, radix, parts_ref)
    product_y(parts_ref, table_ref, mid_ref, radix)
    leaving = []
    upper = upper_lanes((8, LANES))
    for i, begin in enumerate(chunks):
        for x in range(begin, begin + step, 8):
            rows = slice(x, x + 8)
            results = [backward_y(mid_ref, t * across + x, 8, radix) for t in range(times)]
            for a in range(radix):
                for c in range(2):
                    values = [results[t][a][c] for t in range(times)]
                    if packed:
                        one, two = values
                        send_ref[2 * a, c, 0, rows, :] = jnp.where(upper, swap_halves(two), one)
                        send_ref[2 * a + 1, c, 0, rows, :] = jnp.where(upper, two, swap_halves(one))
                    elif width >= LANES:
                        slab, offset = a * LANES // width, a * LANES % width
                        for t in range(times):
                            send_ref[slab, c, t, rows, offset : offset + LANES] = values[t]
                    else:
                        for t in range(times):
                            for piece in range(LANES // width):
                                slab = a * LANES // width + piece
                                lanes = slice(piece * width, (piece + 1) * width)
                                send_ref[slab, c, t, rows, :] = values[t][:, lanes]
        rows = pl.ds(begin, step)
        for j in range(2):
            slabs = pl.ds(j * count, count)
            places = pl.ds(lax.rem(flip + j, 2) * count, count)
            copy = pltpu.make_async_copy(
                send_ref.at[slabs, :, :, rows], send_hbm.at[places, :, :, rows], sem.at[1 + i, j]
            )
            copy.start()
            leaving.append(copy)
    for copy in leaving:
        copy.wait()


def put_x(parts_ref, lanes, start, values):
    step = values[0][0].shape[0]
    for k, (re, im) in enumerate(small_dft(values, -1)):
        for part, (a, b) in enumerate(zip(split3(re), split3(im), strict=True)):
            base = part * 2 * LANES
            parts_ref[k, base + start : base + start + step, lanes] = a
            parts_ref[k, base + LANES + start : base + LANES + start + step, lanes] = b


def product_x(parts_ref, table_ref, out_ref, radix):
    for k in range(radix):
        lefts = []
        for part in range(3):
            re, im = table_ref[k, part, 0], table_ref[k, part, 1]
            lefts.append(jnp.concatenate([re, im], axis=0))
            lefts.append(jnp.concatenate([-im, re], axis=0))
        left = jnp.concatenate(lefts + lefts[:4] + lefts[:2], axis=1)
        high = parts_ref[k, : 2 * LANES]
        middle = parts_ref[k, 2 * LANES : 4 * LANES]
        low = parts_ref[k, 4 * LANES :]
        right = jnp.concatenate([high, high, high, middle, middle, low], axis=0)
        out_ref[k] = jnp.dot(left, right, preferred_element_type=F32)


def get_x(out_ref, lanes, start, step, radix):
    picked = [
        (out_ref[k, start : start + step, lanes], out_ref[k, LANES + start : LANES + start + step, lanes])
        for k in range(radix)
    ]
    return small_dft(picked, 1)


def second_kernel(
    packed, recv_ref, table_ref, density_ref, field_ref, growth_ref, gained_ref, last_growth_ref, last_gained_ref,
    parts_ref, mid_ref,
):
    radix = table_ref.shape[0]
    sources, _, times, across, width = recv_ref.shape
    trans = (radix * LANES) // across
    step = min(16, across)
    total = (sources // trans) * times

    def at(c, t, x):
        place, inner = t // times, t % times
        return recv_ref[place * trans + x // across, c, inner, x % across : x % across + step, :]

    for t in range(total):
        lanes = slice(t * width, (t + 1) * width)
        for start in range(0, LANES, step):
            values = [
                (at(0, t, a * LANES + start), at(1, t, a * LANES + start)) for a in range(radix)
            ]
            put_x(parts_ref, lanes, start, values)
    product_x(parts_ref, table_ref, mid_ref, radix)
    upper = upper_lanes((8, LANES))
    for start in range(0, LANES, 8):
        carry = [None] * radix
        for t in range(total):
            lanes = slice(t * width, (t + 1) * width)
            for a, (re, im) in enumerate(get_x(mid_ref, lanes, start, 8, radix)):
                rows = slice(a * LANES + start, a * LANES + start + 8)
                field_ref[0, t, rows, :] = re
                field_ref[1, t, rows, :] = im
                growth, gained = ionise(re, im, density_ref[rows, :])
                if packed:
                    gained = jnp.where(upper, growth * swap_halves(gained) + gained, gained)
                    growth = jnp.where(upper, growth * swap_halves(growth), growth)
                if carry[a] is not None:
                    gained = growth * carry[a][1] + gained
                    growth = growth * carry[a][0]
                growth_ref[t, rows, :] = growth
                gained_ref[t, rows, :] = gained
                if packed:
                    growth = jnp.where(upper, growth, swap_halves(growth))
                    gained = jnp.where(upper, gained, swap_halves(gained))
                carry[a] = (growth, gained)
        for a in range(radix // 2 if packed else radix):
            rows = slice(a * LANES + start, a * LANES + start + 8)
            growth, gained = carry[a]
            if packed:
                growth = jnp.where(upper, carry[a + radix // 2][0], growth)
                gained = jnp.where(upper, carry[a + radix // 2][1], gained)
            last_growth_ref[rows, :] = growth
            last_gained_ref[rows, :] = gained


def third_kernel(packed, rebuild, leaves, field_ref, growth_ref, gained_ref, table_ref, *refs):
    got_refs = refs[:leaves]
    send_hbm, parts_ref, mid_ref, send_ref, sem = refs[leaves:]

    def enter(start, step):
        got = [ref[start : start + step, :] for ref in got_refs]
        return finish_scan(Z_AXES, rebuild(got), packed)

    radix = table_ref.shape[0]
    _, total, _, width = field_ref.shape
    slabs, _, times, across, _ = send_ref.shape
    trans = (radix * LANES) // across
    step = 16
    upper = upper_lanes((step, LANES))
    for start in range(0, LANES, step):
        entering = []
        for a in range(radix):
            if packed:
                base = (a % (radix // 2)) * LANES + start
                value = enter(base, step)
                other = swap_halves(value)
                first = a < radix // 2
                entering.append(jnp.where(upper, other if first else value, value if first else other))
            else:
                entering.append(enter(a * LANES + start, step))
        for t in range(total):
            lanes = slice(t * width, (t + 1) * width)
            values = []
            for a in range(radix):
                rows = slice(a * LANES + start, a * LANES + start + step)
                electrons = growth_ref[t, rows, :] * entering[a] + gained_ref[t, rows, :]
                values.append(rotate(field_ref[0, t, rows, :], field_ref[1, t, rows, :], electrons))
            put_x(parts_ref, lanes, start, values)
    product_x(parts_ref, table_ref, mid_ref, radix)
    leaving = []
    for t in range(total):
        lanes = slice(t * width, (t + 1) * width)
        place, inner = t // times, t % times
        for start in range(0, LANES, 8):
            for a, pair in enumerate(get_x(mid_ref, lanes, start, 8, radix)):
                x = a * LANES + start
                row = x % across
                for c in range(2):
                    send_ref[place * trans + x // across, c, inner, row : row + 8, :] = pair[c]
        if inner == times - 1:
            block = pl.ds(place * trans, trans)
            copy = pltpu.make_async_copy(send_ref.at[block], send_hbm.at[block], sem.at[place])
            copy.start()
            leaving.append(copy)
    for copy in leaving:
        copy.wait()


def fourth_kernel(
    packed, recv_ref, table_ref, density_ref, field_ref, growth_ref, gained_ref, mine_ref, theirs_ref,
    parts_ref, mid_ref,
):
    radix = table_ref.shape[0]
    _, times, across, _ = field_ref.shape
    width = recv_ref.shape[-1]
    core = lax.axis_index("core")
    step = min(16, across)
    upper = upper_lanes((step, LANES))
    slabs = recv_ref.shape[0]
    flip = lax.rem(lax.axis_index("zh"), 2) * (slabs // 2) if packed else 0

    def part(c, t, x, a):
        rows = slice(x, x + step)
        if packed:
            place = lax.rem(2 * a + flip, slabs)
            one, two = recv_ref[place, c, 0, rows, :], recv_ref[place + 1, c, 0, rows, :]
            if t == 0:
                return jnp.where(upper, swap_halves(two), one)
            return jnp.where(upper, two, swap_halves(one))
        if width >= LANES:
            slab, offset = a * LANES // width, a * LANES % width
            return recv_ref[slab, c, t, rows, offset : offset + LANES]
        pieces = LANES // width
        return jnp.concatenate(
            [recv_ref[a * pieces + p, c, t, rows, :] for p in range(pieces)], axis=1
        )

    for x in range(0, across, step):
        for t in range(times):

            def load(a, x=x, t=t):
                return part(0, t, x, a), part(1, t, x, a)

            forward_y(load, t * across + x, step, radix, parts_ref)
    product_y(parts_ref, table_ref, mid_ref, radix)
    half = across // 2
    for x in range(0, across, 8):
        rows = slice(x, x + 8)
        growth, gained = [None] * radix, [None] * radix
        for t in range(times):
            for a, (re, im) in enumerate(backward_y(mid_ref, t * across + x, 8, radix)):
                lanes = slice(a * LANES, (a + 1) * LANES)
                field_ref[0, t, rows, lanes] = re
                field_ref[1, t, rows, lanes] = im
                decay, source = ionise(re, im, density_ref[rows, lanes])
                if t == 0:
                    growth[a], gained[a] = decay, source
                else:
                    gained[a] = decay * gained[a] + source
                    growth[a] = growth[a] * decay
                growth_ref[t, rows, lanes] = growth[a]
                gained_ref[t, rows, lanes] = gained[a]
    last = times - 1

    def hand_out(own):
        kept, given = slice(own * half, (own + 1) * half), slice((1 - own) * half, (2 - own) * half)
        mine_ref[0] = growth_ref[last, kept, :]
        mine_ref[1] = gained_ref[last, kept, :]
        theirs_ref[0] = growth_ref[last, given, :]
        theirs_ref[1] = gained_ref[last, given, :]

    pl.when(core == 0)(functools.partial(hand_out, 0))
    pl.when(core == 1)(functools.partial(hand_out, 1))


def turn_rows(base, x, field_ref, growth_ref, gained_ref, entering_ref, light_ref, electrons_ref):
    _, times, _, length = field_ref.shape
    rows, out_rows = pl.ds(pl.multiple_of(base + x, 8), 8), slice(x, x + 8)
    entering = entering_ref[out_rows, :]
    for t in range(times):
        results = []
        for a in range(length // LANES):
            lanes = slice(a * LANES, (a + 1) * LANES)
            electrons = growth_ref[t, rows, lanes] * entering[:, lanes] + gained_ref[t, rows, lanes]
            re, im = rotate(field_ref[0, t, rows, lanes], field_ref[1, t, rows, lanes], electrons)
            results.append((re, im, electrons))
        re, im, electrons = (jnp.concatenate(part, axis=1) for part in zip(*results, strict=True))
        light_ref[0, out_rows, t, :] = re
        light_ref[1, out_rows, t, :] = im
        electrons_ref[out_rows, t, :] = electrons


def own_kernel(field_ref, growth_ref, gained_ref, entering_ref, light_ref, electrons_ref):
    half = field_ref.shape[2] // 2
    base = lax.axis_index("core") * half
    for x in range(0, half, 8):
        turn_rows(base, x, field_ref, growth_ref, gained_ref, entering_ref, light_ref, electrons_ref)


def other_kernel(
    field_ref, growth_ref, gained_ref, entering_ref, own_light_ref, own_electrons_ref, light_hbm, electrons_hbm,
    light_ref, electrons_ref, sem,
):
    half = field_ref.shape[2] // 2
    core = lax.axis_index("core")
    base = (1 - core) * half
    leaving = []

    def leave(i, light, electrons, target):
        for copy in (
            pltpu.make_async_copy(light, light_hbm.at[:, target], sem.at[0, i]),
            pltpu.make_async_copy(electrons, electrons_hbm.at[target], sem.at[1, i]),
        ):
            copy.start()
            leaving.append(copy)

    leave(0, own_light_ref, own_electrons_ref, pl.ds(core * half, half))
    step = min(8, half)
    for i, begin in enumerate(range(0, half, step)):
        for x in range(begin, begin + step, 8):
            turn_rows(base, x, field_ref, growth_ref, gained_ref, entering_ref, light_ref, electrons_ref)
        block = pl.ds(begin, step)
        leave(1 + i, light_ref.at[:, block], electrons_ref.at[block], pl.ds(base + begin, step))
    for copy in leaving:
        copy.wait()


def call(kernel, operands, outs, scratch=()):
    return pl.pallas_call(
        kernel,
        out_shape=[jax.ShapeDtypeStruct(shape, kind) for shape, kind, _ in outs],
        in_specs=[spec for _, spec in operands],
        out_specs=[spec for _, _, spec in outs],
        scratch_shapes=list(scratch),
        compiler_params=pltpu.CompilerParams(vmem_limit_bytes=VMEM_LIMIT),
    )(*[array for array, _ in operands])


def in_hbm(array):
    return pltpu.with_memory_space_constraint(array, pltpu.MemorySpace.HBM)


def fuse(function, *arrays):
    outs = jax.eval_shape(function, *arrays)

    def kernel(*refs):
        results = function(*[ref[...] for ref in refs[: len(arrays)]])
        for ref, result in zip(refs[len(arrays) :], results, strict=True):
            ref[...] = result

    return call(
        kernel,
        [(array, VMEM_SPEC) for array in arrays],
        [(out.shape, out.dtype, VMEM_SPEC) for out in outs],
    )


def both_ways(pairs):
    return pairs + [(b, a) for a, b in pairs]


def widen(pairs):
    return [(2 * a + i, 2 * b + (i + a + b) % 2) for a, b in pairs for i in range(2)]


def scan_levels(axis, growth, gained, paired):
    count = lax.axis_size(axis) // (2 if paired else 1)
    kept = []
    size = 1
    while size < count:
        need_growth = 2 * size < count
        got_gained, got_growth = [], []
        for reach in range(1, size + 1):
            pairs = [
                (b + size - 1, b + size - 1 + reach)
                for b in range(0, count, 2 * size)
                if b + size - 1 + reach < count
            ]
            spread = widen if paired else list
            got_gained.append(lax.ppermute(gained, axis, spread(both_ways(pairs))))
            if need_growth:
                later = [pair for pair in pairs if pair[0] >= 2 * size]
                got_growth.append(lax.ppermute(growth, axis, spread(both_ways(later))))
        kept.append((got_gained, got_growth))
        if need_growth and 4 * size < count:

            def both(growth, gained, *got):
                new_gained, new_growth = sum(got[: len(got) // 2]), sum(got[len(got) // 2 :])
                return growth * new_growth, growth * new_gained + gained

            growth, gained = fuse(both, growth, gained, *got_gained, *got_growth)
        elif need_growth:
            (gained,) = fuse(
                lambda growth, gained, *got: (growth * sum(got) + gained,), growth, gained, *got_gained
            )
        size *= 2
    return kept


def finish_scan(axis, levels, paired):
    place = lax.axis_index(axis) // (2 if paired else 1)
    before_growth = before_gained = None
    for level, (got_gained, got_growth) in enumerate(levels):
        new_gained = sum(got_gained)
        upper = (place // 2**level) % 2 == 1
        if before_gained is None:
            before_gained = jnp.where(upper, new_gained, 0.0)
        else:
            new_gained = before_growth * new_gained + before_gained
            before_gained = jnp.where(upper, new_gained, before_gained)
        if got_growth:
            new_growth = sum(got_growth)
            if before_growth is None:
                before_growth = jnp.where(upper, new_growth, 1.0)
            else:
                before_growth = jnp.where(upper, before_growth * new_growth, before_growth)
    return before_gained


def flatten(levels):
    leaves, tree = jax.tree.flatten(levels)
    return leaves, lambda values: jax.tree.unflatten(tree, values)


def local(packed, light_field, gas_density, phase_x, phase_y):
    width_x, width_y = phase_x.shape[0], phase_y.shape[0]
    radix_x, radix_y = width_x // LANES, width_y // LANES
    _, across, times, _ = light_field.shape
    group = GROUP[packed]
    slabs = lax.axis_size(group)
    width = width_y // slabs
    slab = lax.axis_index(group)
    if packed:
        slab = lax.rem(slab + lax.rem(lax.axis_index("zh"), 2) * (slabs // 2), slabs)
    trans = lax.axis_size("trans")
    density_y = lax.dynamic_slice_in_dim(gas_density, slab * width, width, 1)
    density_x = lax.dynamic_slice_in_dim(gas_density, lax.axis_index("trans") * across, across, 0)
    density_y, density_x = lax.optimization_barrier((density_y, density_x))
    if packed:
        density_y = jnp.concatenate([density_y] * times, axis=1)
        sent_shape = (slabs, 2, 1, across, times * width)
    else:
        sent_shape = (slabs, 2, times, across, width)
    inner, lanes = sent_shape[2], sent_shape[4]
    total = (slabs // trans) * inner
    rows = times * across

    def vmem(*shapes):
        return [(shape, F32, VMEM_SPEC) for shape in shapes]

    scratch_y = [
        pltpu.VMEM((radix_y, 3, rows, 2 * LANES), BF16),
        pltpu.VMEM((radix_y, rows, 2 * LANES), F32),
    ]
    scratch_x = [
        pltpu.VMEM((radix_x, 6 * LANES, total * lanes), BF16),
        pltpu.VMEM((radix_x, 2 * LANES, total * lanes), F32),
    ]
    table_y_shape = (radix_y, 3, 2, LANES, LANES)
    phase_y = phase_y.reshape(radix_y, LANES)
    (table_x,) = call(
        functools.partial(table_kernel, -1),
        [(phase_x.reshape(radix_x, LANES), VMEM_SPEC)],
        [((radix_x, 3, 2, LANES, LANES), BF16, VMEM_SPEC)],
    )
    (sent,) = call(
        functools.partial(first_kernel, packed),
        [(in_hbm(light_field), HBM_SPEC), (in_hbm(phase_y), HBM_SPEC)],
        [(sent_shape, F32, HBM_SPEC)],
        [pltpu.VMEM(table_y_shape, BF16)]
        + scratch_y
        + [
            pltpu.VMEM(light_field.shape, F32),
            pltpu.VMEM((2, times, across, width_y), F32),
            pltpu.VMEM(phase_y.shape, F32),
            pltpu.VMEM(sent_shape, F32),
            pltpu.SemaphoreType.DMA((1 + across // min(16, across), 2)),
        ],
    )
    received = lax.all_to_all(sent, group, 0, 0, tiled=True)
    cells = (width_x, lanes)
    last = (width_x // 2, lanes) if packed else cells
    field, growth, gained, last_growth, last_gained = call(
        functools.partial(second_kernel, packed),
        [(received, VMEM_SPEC), (table_x, VMEM_SPEC), (density_y, VMEM_SPEC)],
        vmem((2, total) + cells, (total,) + cells, (total,) + cells, last, last),
        scratch_x,
    )
    levels = scan_levels(Z_AXES, last_growth, last_gained, packed)
    leaves, rebuild = flatten(levels)
    (table_y,) = call(
        functools.partial(table_kernel, 1),
        [(phase_y, VMEM_SPEC), (last_gained, VMEM_SPEC)],
        [(table_y_shape, BF16, VMEM_SPEC)],
    )
    table_y, leaves = lax.optimization_barrier((table_y, leaves))
    (sent,) = call(
        functools.partial(third_kernel, packed, rebuild, len(leaves)),
        [(array, VMEM_SPEC) for array in (field, growth, gained, table_x, *leaves)],
        [(sent_shape, F32, HBM_SPEC)],
        scratch_x + [pltpu.VMEM(sent_shape, F32), pltpu.SemaphoreType.DMA((slabs // trans,))],
    )
    received = lax.all_to_all(sent, group, 0, 0, tiled=True)
    cells = (across, width_y)
    half = (2, across // 2, width_y)
    field, growth, gained, mine, theirs = call(
        functools.partial(fourth_kernel, packed),
        [(received, VMEM_SPEC), (table_y, VMEM_SPEC), (density_x, VMEM_SPEC)],
        vmem((2, times) + cells, (times,) + cells, (times,) + cells, half, half),
        scratch_y,
    )
    swap = [(0, 1), (1, 0)]
    other = lax.ppermute(theirs, "core", swap)

    def ordered(mine, other):
        first = lax.axis_index("core") == 0
        early = [jnp.where(first, mine[i], other[i]) for i in range(2)]
        late = [jnp.where(first, other[i], mine[i]) for i in range(2)]
        return early, late

    def chip_map(mine, other):
        early, late = ordered(mine, other)
        return late[0] * early[0], late[0] * early[1] + late[1]

    levels = scan_levels(Z_AXES, *fuse(chip_map, mine, other), False)
    leaves, rebuild = flatten(levels)

    def hand_over(mine, other, *got):
        early, _ = ordered(mine, other)
        first = lax.axis_index("core") == 0
        entering = finish_scan(Z_AXES, rebuild(got), False)
        halfway = early[0] * entering + early[1]
        return jnp.where(first, entering, halfway), jnp.where(first, halfway, entering)

    kept, given = fuse(hand_over, mine, other, *leaves)
    given = lax.ppermute(given, "core", swap)
    rows = across // 2
    operands = [(array, VMEM_SPEC) for array in (field, growth, gained)]
    light_half, electrons_half = (2, rows, times, width_y), (rows, times, width_y)
    own = call(own_kernel, operands + [(kept, VMEM_SPEC)], vmem(light_half, electrons_half))
    return call(
        other_kernel,
        operands + [(array, VMEM_SPEC) for array in (given, *own)],
        [(light_field.shape, F32, HBM_SPEC), ((across, times, width_y), F32, HBM_SPEC)],
        [
            pltpu.VMEM(light_half, F32),
            pltpu.VMEM(electrons_half, F32),
            pltpu.SemaphoreType.DMA((2, 1 + rows // min(8, rows))),
        ],
    )


def solution(mesh):
    slabs, trans = mesh.shape["tm"], mesh.shape["trans"]

    def run(light_field, gas_density, phase_x, phase_y):
        times = light_field.shape[2] // slabs
        width = phase_y.shape[0] // (trans * 4)
        packed = (
            slabs % 4 == 0
            and slabs > 4
            and times == 2
            and times * width == LANES
            and phase_x.shape[0] % (2 * LANES) == 0
        )
        pair = 2 if packed else 1
        split = Mesh(
            mesh.devices.reshape(slabs // (2 * pair), pair, 2, trans), ("zh", "zl", "core", "trans")
        )
        time_axes = ("zh", "zl", "core")
        placed = (P(None, "trans", time_axes, None), P(), P(), P())
        return jax.shard_map(
            functools.partial(local, packed),
            mesh=split,
            in_specs=placed,
            out_specs=(P(None, "trans", time_axes, None), P("trans", time_axes, None)),
            check_vma=False,
        )(light_field, gas_density, phase_x, phase_y)

    return run
```

```python
import functools
import math

import jax
import jax.numpy as jnp
from jax import lax
from jax.experimental import pallas as pl
from jax.experimental.pallas import tpu as pltpu
from jax.sharding import Mesh
from jax.sharding import PartitionSpec as P

PHOTONS = 8
STEPS = 2
RATE_COEF = 1.8e-08
RECOMB = 0.02
KERR_COEF = 0.3
PLASMA = 4.0
LANES = 128
Z_AXES = ("zh", "zl")
GROUP = ("zl", "trans")
VMEM_LIMIT = 16 * 1024 * 1024
F32 = jnp.float32
BF16 = jnp.bfloat16
VMEM_SPEC = pl.BlockSpec(memory_space=pltpu.VMEM)
ANY_SPEC = pl.BlockSpec(memory_space=pl.ANY)
HBM_SPEC = pl.BlockSpec(memory_space=pltpu.MemorySpace.HBM)


def sincos(quarter):
    turns = jnp.floor(quarter * (2.0 / math.pi) + 0.5)
    rest = quarter - turns * 1.5703125
    rest = rest - turns * 4.837512969970703125e-4
    rest = rest - turns * 7.54978995489188e-8
    square = rest * rest
    sine = ((-1.9515295891e-4 * square + 8.3321608736e-3) * square - 1.6666654611e-1) * square
    sine = sine * rest + rest
    cosine = (2.443315711809948e-5 * square - 1.388731625493765e-3) * square
    cosine = (cosine + 4.166664568298827e-2) * (square * square) - 0.5 * square + 1.0
    for _ in range(2):
        twice = sine + sine
        sine, cosine = twice * cosine, 1.0 - twice * sine
    return sine, cosine


def split3(value):
    high = value.astype(BF16)
    rest = value - high.astype(F32)
    middle = rest.astype(BF16)
    low = (rest - middle.astype(F32)).astype(BF16)
    return high, middle, low


def turned(value, order, position, sign):
    re, im = value
    eighth = (position * 8) // order
    if (position * 8) % order == 0 and eighth % 2 == 0:
        quarter = (eighth // 2 * sign) % 4
        return ((re, im), (-im, re), (-re, -im), (im, -re))[quarter]
    angle = sign * 2.0 * math.pi * position / order
    c, s = math.cos(angle), math.sin(angle)
    if (position * 8) % order == 0:
        root = math.sqrt(0.5)
        sc, ss = math.copysign(1, c), math.copysign(1, s)
        one = re - im if sc == ss else re + im
        two = re + im if sc == ss else re - im
        new_re = one * (root * sc)
        new_im = two * (root * ss) if sc == ss else two * (root * ss)
        return (new_re, new_im)
    return (re * c - im * s, re * s + im * c)


def small_dft(values, sign):
    count = len(values)
    if count == 1:
        return values
    even = small_dft(values[0::2], sign)
    odd = small_dft(values[1::2], sign)
    upper, lower = [], []
    for k in range(count // 2):
        other = turned(odd[k], count, k, sign)
        upper.append((even[k][0] + other[0], even[k][1] + other[1]))
        lower.append((even[k][0] - other[0], even[k][1] - other[1]))
    return upper + lower


def ionise(re, im, density):
    intensity = re * re + im * im
    power = intensity * intensity
    power = power * power
    rate = RATE_COEF * (power * power)
    loss = rate + RECOMB
    decay = jnp.exp(-loss)
    source = (1.0 - decay) * density * rate / loss
    return decay, source


def rotate(re, im, electrons):
    intensity = re * re + im * im
    sine, cosine = sincos((0.25 * KERR_COEF) * intensity - (0.25 * PLASMA) * electrons)
    return re * cosine - im * sine, re * sine + im * cosine


def wave(shape, order, sign):
    product = lax.broadcasted_iota(jnp.int32, shape, 0) * lax.broadcasted_iota(jnp.int32, shape, 1)
    sine, cosine = sincos((product % order).astype(F32) * (0.5 * math.pi / order))
    return cosine, sign * sine


def toeplitz_blocks(phase, radix, sign):
    length = radix * LANES
    waves = jnp.concatenate(wave((LANES, LANES), length, sign), axis=1)
    block_re, block_im = wave((radix, LANES), radix, sign)
    block_re, block_im = block_re * (1.0 / length), block_im * (1.0 / length)
    sine, cosine = sincos(0.25 * phase)
    lane = lax.broadcasted_iota(jnp.int32, phase.shape, 1) % radix
    picked = [jnp.where(lane == k, part, 0.0) for part in (cosine, sine) for k in range(radix)]
    spectrum = jnp.dot(
        jnp.concatenate(picked, axis=0),
        waves,
        precision=lax.Precision.HIGHEST,
        preferred_element_type=F32,
    )
    half = radix * radix
    row = lax.broadcasted_iota(jnp.int32, (LANES, LANES), 0)
    column = lax.broadcasted_iota(jnp.int32, (LANES, LANES), 1)
    direct = column >= row
    blocks = []
    for k in range(radix):
        ours = slice(k * radix, (k + 1) * radix)
        theirs = slice(half + k * radix, half + (k + 1) * radix)
        re = spectrum[ours, :LANES] - spectrum[theirs, LANES:]
        im = spectrum[ours, LANES:] + spectrum[theirs, :LANES]
        full_re = jnp.sum(re * block_re - im * block_im, axis=0, keepdims=True)
        full_im = jnp.sum(re * block_im + im * block_re, axis=0, keepdims=True)
        spread_re = jnp.broadcast_to(full_re, (LANES, LANES))
        spread_im = jnp.broadcast_to(full_im, (LANES, LANES))
        rolled = (
            pltpu.roll(spread_re, 0, 1, stride=1, stride_axis=0),
            pltpu.roll(spread_im, 0, 1, stride=1, stride_axis=0),
        )
        wrapped = turned(rolled, radix, k, -sign)
        blocks.append(
            (jnp.where(direct, rolled[0], wrapped[0]), jnp.where(direct, rolled[1], wrapped[1]))
        )
    return blocks


def store_parts(table_ref, blocks):
    for k, (re, im) in enumerate(blocks):
        for part, (a, b) in enumerate(zip(split3(re), split3(im), strict=True)):
            table_ref[k, part, 0] = a
            table_ref[k, part, 1] = b


def table_kernel(sign, phase_ref, *refs):
    table_ref = refs[-1]
    store_parts(table_ref, toeplitz_blocks(phase_ref[...], table_ref.shape[0], sign))


def forward_y(load, start, step, radix, parts_ref):
    blocks = small_dft([load(a) for a in range(radix)], -1)
    for k, (re, im) in enumerate(blocks):
        for part, (a, b) in enumerate(zip(split3(re), split3(im), strict=True)):
            parts_ref[k, part, start : start + step, :LANES] = a
            parts_ref[k, part, start : start + step, LANES:] = b


def product_y(parts_ref, table_ref, out_ref, radix):
    for k in range(radix):
        high, middle, low = parts_ref[k, 0], parts_ref[k, 1], parts_ref[k, 2]
        left = jnp.concatenate([high, high, high, middle, middle, low], axis=1)
        rights = []
        for part in range(3):
            re, im = table_ref[k, part, 0], table_ref[k, part, 1]
            rights.append(jnp.concatenate([re, im], axis=1))
            rights.append(jnp.concatenate([-im, re], axis=1))
        right = jnp.concatenate(rights + rights[:4] + rights[:2], axis=0)
        out_ref[k] = jnp.dot(left, right, preferred_element_type=F32)


def backward_y(out_ref, start, step, radix):
    picked = [
        (out_ref[k, start : start + step, :LANES], out_ref[k, start : start + step, LANES:])
        for k in range(radix)
    ]
    return small_dft(picked, 1)


def member_and_flip(slabs):
    turned_pair = lax.rem(lax.axis_index("zh"), 2)
    return lax.axis_index(GROUP), turned_pair * (slabs // 2)


def give_out(send_ref, out_refs, flip):
    member, _ = member_and_flip(len(out_refs))
    for k, out_ref in enumerate(out_refs):
        out_ref[...] = send_ref[member ^ k ^ flip]


def take_in(recv_ref, in_refs, flip):
    member, _ = member_and_flip(len(in_refs))
    for k, in_ref in enumerate(in_refs):
        recv_ref[member ^ k ^ flip] = in_ref[...]


def first_kernel(light_hbm, phase_hbm, *refs):
    out_refs = refs[:-8]
    table_ref, parts_ref, mid_ref, light_ref, rows_ref, phase_ref, send_ref, sem = refs[-8:]
    radix = table_ref.shape[0]
    _, across, times, _ = light_ref.shape
    width = send_ref.shape[-1]
    step = min(16, across)
    chunks = range(0, across, step)
    phase_copy = pltpu.make_async_copy(phase_hbm, phase_ref, sem.at[0])
    phase_copy.start()
    arriving = []
    for i, x in enumerate(chunks):
        rows = pl.ds(x, step)
        copy = pltpu.make_async_copy(light_hbm.at[:, rows], light_ref.at[:, rows], sem.at[1 + i])
        copy.start()
        arriving.append(copy)
    phase_copy.wait()
    store_parts(table_ref, toeplitz_blocks(phase_ref[...], radix, 1))
    for copy, x in zip(arriving, chunks, strict=True):
        copy.wait()
        for t in range(times):
            for c in range(2):
                for start in range(x, x + step, 8):
                    rows_ref[c, t, start : start + 8, :] = light_ref[c, start : start + 8, t, :]

            def load(a, x=x, t=t):
                lanes = slice(a * LANES, (a + 1) * LANES)
                rows = slice(x, x + step)
                return rows_ref[0, t, rows, lanes], rows_ref[1, t, rows, lanes]

            forward_y(load, t * across + x, step, radix, parts_ref)
    product_y(parts_ref, table_ref, mid_ref, radix)
    for t in range(times):
        for x in range(0, across, 8):
            rows = slice(x, x + 8)
            for a, pair in enumerate(backward_y(mid_ref, t * across + x, 8, radix)):
                for c in range(2):
                    if width >= LANES:
                        slab, offset = a * LANES // width, a * LANES % width
                        send_ref[slab, c, t, rows, offset : offset + LANES] = pair[c]
                    else:
                        for piece in range(LANES // width):
                            slab = a * LANES // width + piece
                            lanes = slice(piece * width, (piece + 1) * width)
                            send_ref[slab, c, t, rows, :] = pair[c][:, lanes]
    give_out(send_ref, out_refs, member_and_flip(len(out_refs))[1])


def put_x(parts_ref, lanes, start, values):
    step = values[0][0].shape[0]
    for k, (re, im) in enumerate(small_dft(values, -1)):
        for part, (a, b) in enumerate(zip(split3(re), split3(im), strict=True)):
            base = part * 2 * LANES
            parts_ref[k, base + start : base + start + step, lanes] = a
            parts_ref[k, base + LANES + start : base + LANES + start + step, lanes] = b


def product_x(parts_ref, table_ref, out_ref, radix):
    for k in range(radix):
        lefts = []
        for part in range(3):
            re, im = table_ref[k, part, 0], table_ref[k, part, 1]
            lefts.append(jnp.concatenate([re, im], axis=0))
            lefts.append(jnp.concatenate([-im, re], axis=0))
        left = jnp.concatenate(lefts + lefts[:4] + lefts[:2], axis=1)
        high = parts_ref[k, : 2 * LANES]
        middle = parts_ref[k, 2 * LANES : 4 * LANES]
        low = parts_ref[k, 4 * LANES :]
        right = jnp.concatenate([high, high, high, middle, middle, low], axis=0)
        out_ref[k] = jnp.dot(left, right, preferred_element_type=F32)


def get_x(out_ref, lanes, start, step, radix):
    picked = [
        (out_ref[k, start : start + step, lanes], out_ref[k, LANES + start : LANES + start + step, lanes])
        for k in range(radix)
    ]
    return small_dft(picked, 1)


def second_kernel(table_ref, density_ref, *refs):
    in_refs = refs[:-7]
    field_ref, growth_ref, gained_ref, theirs_ref, recv_ref, parts_ref, mid_ref = refs[-7:]
    radix = table_ref.shape[0]
    sources, _, times, across, width = recv_ref.shape
    trans = (radix * LANES) // across
    step = min(16, across)
    total = (sources // trans) * times
    take_in(recv_ref, in_refs, 0)

    def at(c, t, x):
        place, inner = t // times, t % times
        return recv_ref[place * trans + x // across, c, inner, x % across : x % across + step, :]

    for t in range(total):
        lanes = slice(t * width, (t + 1) * width)
        for start in range(0, LANES, step):
            values = [
                (at(0, t, a * LANES + start), at(1, t, a * LANES + start)) for a in range(radix)
            ]
            put_x(parts_ref, lanes, start, values)
    product_x(parts_ref, table_ref, mid_ref, radix)
    for start in range(0, LANES, 8):
        carry = [None] * radix
        for t in range(total):
            lanes = slice(t * width, (t + 1) * width)
            for a, (re, im) in enumerate(get_x(mid_ref, lanes, start, 8, radix)):
                rows = slice(a * LANES + start, a * LANES + start + 8)
                field_ref[0, t, rows, :] = re
                field_ref[1, t, rows, :] = im
                growth, gained = ionise(re, im, density_ref[rows, :])
                if t % times:
                    gained = growth * carry[a][1] + gained
                    growth = growth * carry[a][0]
                growth_ref[t, rows, :] = growth
                gained_ref[t, rows, :] = gained
                carry[a] = (growth, gained)
    hand_partner(growth_ref, gained_ref, theirs_ref)


def third_kernel(field_ref, growth_ref, gained_ref, table_ref, kept_ref, given_ref, *refs):
    out_refs = refs[:-4]
    entering_ref, parts_ref, mid_ref, send_ref = refs[-4:]
    radix = table_ref.shape[0]
    _, total, _, width = field_ref.shape
    slabs, _, times, across, _ = send_ref.shape
    trans = (radix * LANES) // across
    half = radix * LANES // 2
    core = lax.axis_index("core")
    entering_ref[:, pl.ds(pl.multiple_of(core * half, 8), half)] = kept_ref[...]
    entering_ref[:, pl.ds(pl.multiple_of((1 - core) * half, 8), half)] = given_ref[...]
    step = 16
    for start in range(0, LANES, step):
        for t in range(total):
            lanes = slice(t * width, (t + 1) * width)
            values = []
            for a in range(radix):
                rows = slice(a * LANES + start, a * LANES + start + step)
                electrons = growth_ref[t, rows, :] * entering_ref[t // times, rows, :] + gained_ref[t, rows, :]
                values.append(rotate(field_ref[0, t, rows, :], field_ref[1, t, rows, :], electrons))
            put_x(parts_ref, lanes, start, values)
    product_x(parts_ref, table_ref, mid_ref, radix)
    for t in range(total):
        lanes = slice(t * width, (t + 1) * width)
        place, inner = t // times, t % times
        for start in range(0, LANES, 8):
            for a, pair in enumerate(get_x(mid_ref, lanes, start, 8, radix)):
                x = a * LANES + start
                row = x % across
                for c in range(2):
                    send_ref[place * trans + x // across, c, inner, row : row + 8, :] = pair[c]
    give_out(send_ref, out_refs, 0)


def fourth_kernel(table_ref, density_ref, *refs):
    in_refs = refs[:-7]
    field_ref, growth_ref, gained_ref, theirs_ref, recv_ref, parts_ref, mid_ref = refs[-7:]
    radix = table_ref.shape[0]
    _, times, across, _ = field_ref.shape
    width = recv_ref.shape[-1]
    step = min(16, across)
    take_in(recv_ref, in_refs, member_and_flip(len(in_refs))[1])

    def part(c, t, x, a):
        rows = slice(x, x + step)
        if width >= LANES:
            slab, offset = a * LANES // width, a * LANES % width
            return recv_ref[slab, c, t, rows, offset : offset + LANES]
        pieces = LANES // width
        return jnp.concatenate(
            [recv_ref[a * pieces + p, c, t, rows, :] for p in range(pieces)], axis=1
        )

    for x in range(0, across, step):
        for t in range(times):

            def load(a, x=x, t=t):
                return part(0, t, x, a), part(1, t, x, a)

            forward_y(load, t * across + x, step, radix, parts_ref)
    product_y(parts_ref, table_ref, mid_ref, radix)
    for x in range(0, across, 8):
        rows = slice(x, x + 8)
        carry = [None] * radix
        for t in range(times):
            for a, (re, im) in enumerate(backward_y(mid_ref, t * across + x, 8, radix)):
                lanes = slice(a * LANES, (a + 1) * LANES)
                field_ref[0, t, rows, lanes] = re
                field_ref[1, t, rows, lanes] = im
                growth, gained = ionise(re, im, density_ref[rows, lanes])
                if t:
                    gained = growth * carry[a][1] + gained
                    growth = growth * carry[a][0]
                growth_ref[t, rows, lanes] = growth
                gained_ref[t, rows, lanes] = gained
                carry[a] = (growth, gained)
    hand_partner(growth_ref, gained_ref, theirs_ref)


def last_maps(growth_ref, gained_ref, blocks, half, side):
    times = growth_ref.shape[0] // blocks
    rows = pl.ds(pl.multiple_of(side * half, 8), half)
    ends = [block * times + times - 1 for block in range(blocks)]
    return [(growth_ref[t, rows, :], gained_ref[t, rows, :]) for t in ends]


def hand_partner(growth_ref, gained_ref, theirs_ref):
    blocks, _, half, _ = theirs_ref.shape
    core = lax.axis_index("core")
    for block, maps in enumerate(last_maps(growth_ref, gained_ref, blocks, half, 1 - core)):
        for i in range(2):
            theirs_ref[block, i] = maps[i]


def in_order(growth_ref, gained_ref, other_ref):
    blocks, _, half, _ = other_ref.shape
    core = lax.axis_index("core")
    first = core == 0
    ordered = []
    for block, maps in enumerate(last_maps(growth_ref, gained_ref, blocks, half, core)):
        other = other_ref[block, 0], other_ref[block, 1]
        ordered.append([jnp.where(first, a, b) for a, b in zip(maps, other, strict=True)])
        ordered.append([jnp.where(first, b, a) for a, b in zip(maps, other, strict=True)])
    return ordered


def whole_map_kernel(growth_ref, gained_ref, other_ref, out_gained_ref, out_growth_ref=None):
    growth, gained = None, None
    for a, b in in_order(growth_ref, gained_ref, other_ref):
        growth, gained = (a, b) if growth is None else (growth * a, a * gained + b)
    out_gained_ref[...] = gained
    if out_growth_ref is not None:
        out_growth_ref[...] = growth


def hand_over_kernel(paired, rebuild, growth_ref, gained_ref, other_ref, *refs):
    kept_ref, given_ref = refs[-2:]
    entering = finish_scan(Z_AXES, rebuild([ref[...] for ref in refs[:-2]]), paired)
    before = []
    for a, b in in_order(growth_ref, gained_ref, other_ref):
        before.append(entering)
        entering = a * entering + b
    first = lax.axis_index("core") == 0
    for block in range(kept_ref.shape[0]):
        early, late = before[2 * block : 2 * block + 2]
        kept_ref[block] = jnp.where(first, early, late)
        given_ref[block] = jnp.where(first, late, early)


def turn_rows(base, x, field_ref, growth_ref, gained_ref, entering_ref, light_ref, electrons_ref):
    _, times, _, length = field_ref.shape
    rows, out_rows = pl.ds(pl.multiple_of(base + x, 8), 8), slice(x, x + 8)
    entering = entering_ref[0, out_rows, :]
    for t in range(times):
        results = []
        for a in range(length // LANES):
            lanes = slice(a * LANES, (a + 1) * LANES)
            electrons = growth_ref[t, rows, lanes] * entering[:, lanes] + gained_ref[t, rows, lanes]
            re, im = rotate(field_ref[0, t, rows, lanes], field_ref[1, t, rows, lanes], electrons)
            results.append((re, im, electrons))
        re, im, electrons = (jnp.concatenate(part, axis=1) for part in zip(*results, strict=True))
        light_ref[0, out_rows, t, :] = re
        light_ref[1, out_rows, t, :] = im
        electrons_ref[out_rows, t, :] = electrons


def own_kernel(field_ref, growth_ref, gained_ref, entering_ref, light_ref, electrons_ref):
    half = field_ref.shape[2] // 2
    base = lax.axis_index("core") * half
    for x in range(0, half, 8):
        turn_rows(base, x, field_ref, growth_ref, gained_ref, entering_ref, light_ref, electrons_ref)


def other_kernel(
    field_ref, growth_ref, gained_ref, entering_ref, own_light_ref, own_electrons_ref, light_hbm, electrons_hbm,
    light_ref, electrons_ref, sem,
):
    half = field_ref.shape[2] // 2
    core = lax.axis_index("core")
    base = (1 - core) * half
    leaving = []

    def leave(i, light, electrons, target):
        for copy in (
            pltpu.make_async_copy(light, light_hbm.at[:, target], sem.at[0, i]),
            pltpu.make_async_copy(electrons, electrons_hbm.at[target], sem.at[1, i]),
        ):
            copy.start()
            leaving.append(copy)

    leave(0, own_light_ref, own_electrons_ref, pl.ds(core * half, half))
    step = min(8, half)
    for i, begin in enumerate(range(0, half, step)):
        for x in range(begin, begin + step, 8):
            turn_rows(base, x, field_ref, growth_ref, gained_ref, entering_ref, light_ref, electrons_ref)
        block = pl.ds(begin, step)
        leave(1 + i, light_ref.at[:, block], electrons_ref.at[block], pl.ds(base + begin, step))
    for copy in leaving:
        copy.wait()


def call(kernel, operands, outs, scratch=()):
    return pl.pallas_call(
        kernel,
        out_shape=[jax.ShapeDtypeStruct(shape, kind) for shape, kind, _ in outs],
        in_specs=[spec for _, spec in operands],
        out_specs=[spec for _, _, spec in outs],
        scratch_shapes=list(scratch),
        compiler_params=pltpu.CompilerParams(vmem_limit_bytes=VMEM_LIMIT),
    )(*[array for array, _ in operands])


def in_hbm(array):
    return pltpu.with_memory_space_constraint(array, pltpu.MemorySpace.HBM)


def fuse(function, *arrays):
    outs = jax.eval_shape(function, *arrays)

    def kernel(*refs):
        results = function(*[ref[...] for ref in refs[: len(arrays)]])
        for ref, result in zip(refs[len(arrays) :], results, strict=True):
            ref[...] = result

    return call(
        kernel,
        [(array, VMEM_SPEC) for array in arrays],
        [(out.shape, out.dtype, VMEM_SPEC) for out in outs],
    )


def widen(pairs):
    return [(2 * a + i, 2 * b + (i + a + b) % 2) for a, b in pairs for i in range(2)]


def scan_levels(axis, gained, growth, paired):
    count = lax.axis_size(axis) // (2 if paired else 1)
    levels = []
    size = 1
    while size < count:
        pairs = [(i, i // (2 * size) * 2 * size + 2 * size - 1 - i % (2 * size)) for i in range(count)]
        pairs = widen(pairs) if paired else pairs
        got = [lax.ppermute(gained, axis, pairs)]
        if 2 * size < count:
            got.append(lax.ppermute(growth, axis, pairs))

            def join(growth, gained, got_gained, got_growth, size=size):
                upper = (lax.axis_index(axis) // (2 if paired else 1) // size) % 2 == 1
                later_growth = jnp.where(upper, growth, got_growth)
                early, late = jnp.where(upper, got_gained, gained), jnp.where(upper, gained, got_gained)
                results = (later_growth * early + late, growth * got_growth)
                return results if 4 * size < count else results[:1]

            gained, *rest = fuse(join, growth, gained, *got)
            growth = rest[0] if rest else None
        levels.append(got)
        size *= 2
    return levels


def finish_scan(axis, levels, paired):
    place = lax.axis_index(axis) // (2 if paired else 1)
    before_growth = before_gained = None
    for level, got in enumerate(levels):
        upper = (place // 2**level) % 2 == 1
        new_gained = got[0]
        if before_gained is None:
            before_gained = jnp.where(upper, new_gained, 0.0)
        else:
            new_gained = before_growth * new_gained + before_gained
            before_gained = jnp.where(upper, new_gained, before_gained)
        if len(got) > 1:
            new_growth = got[1] if before_growth is None else before_growth * got[1]
            before_growth = jnp.where(upper, new_growth, 1.0 if before_growth is None else before_growth)
    return before_gained


def flatten(levels):
    leaves, tree = jax.tree.flatten(levels)
    return leaves, lambda values: jax.tree.unflatten(tree, values)


def swap_cores(array):
    return lax.ppermute(array, "core", [(0, 1), (1, 0)])


def exchange(blocks):
    count = len(blocks)
    moved = {
        k: lax.ppermute(blocks[k], GROUP, [(m, m ^ k) for m in range(count)])
        for k in range(count - 1, 0, -1)
    }
    return [blocks[0]] + [moved[k] for k in range(1, count)]


def entering_density(growth, gained, theirs, paired):
    blocks, _, half, lanes = theirs.shape
    other = swap_cores(theirs)
    maps = [(array, VMEM_SPEC) for array in (growth, gained, other)]
    one = ((half, lanes), F32, VMEM_SPEC)
    single = lax.axis_size(Z_AXES) // (2 if paired else 1) <= 2
    whole = call(whole_map_kernel, maps, [one] if single else [one, one])
    levels = scan_levels(Z_AXES, whole[0], None if single else whole[1], paired)
    leaves, rebuild = flatten(levels)
    both = ((blocks, half, lanes), F32, VMEM_SPEC)
    kept, given = call(
        functools.partial(hand_over_kernel, paired, rebuild),
        maps + [(leaf, VMEM_SPEC) for leaf in leaves],
        [both, both],
    )
    return kept, swap_cores(given)


def local(light_field, gas_density, phase_x, phase_y):
    width_x, width_y = phase_x.shape[0], phase_y.shape[0]
    radix_x, radix_y = width_x // LANES, width_y // LANES
    _, across, times, _ = light_field.shape
    trans, slabs = lax.axis_size("trans"), lax.axis_size(GROUP)
    blocks = slabs // trans
    width = width_y // slabs
    member, flip = member_and_flip(slabs)
    density_y = lax.dynamic_slice_in_dim(gas_density, (member ^ flip) * width, width, 1)
    density_x = lax.dynamic_slice_in_dim(gas_density, lax.axis_index("trans") * across, across, 0)
    density_y, density_x = lax.optimization_barrier((density_y, density_x))
    piece = (2, times, across, width)
    sent_shape = (slabs,) + piece
    total = blocks * times
    rows = times * across

    def vmem(*shapes):
        return [(shape, F32, VMEM_SPEC) for shape in shapes]

    def put(*arrays):
        return [(array, VMEM_SPEC) for array in arrays]

    scratch_y = [
        pltpu.VMEM((radix_y, 3, rows, 2 * LANES), BF16),
        pltpu.VMEM((radix_y, rows, 2 * LANES), F32),
    ]
    scratch_x = [
        pltpu.VMEM((radix_x, 6 * LANES, total * width), BF16),
        pltpu.VMEM((radix_x, 2 * LANES, total * width), F32),
    ]
    table_y_shape = (radix_y, 3, 2, LANES, LANES)
    phase_y = phase_y.reshape(radix_y, LANES)
    (table_x,) = call(
        functools.partial(table_kernel, -1),
        put(phase_x.reshape(radix_x, LANES)),
        [((radix_x, 3, 2, LANES, LANES), BF16, VMEM_SPEC)],
    )
    sent = call(
        first_kernel,
        [(in_hbm(light_field), HBM_SPEC), (in_hbm(phase_y), HBM_SPEC)],
        vmem(*[piece] * slabs),
        [pltpu.VMEM(table_y_shape, BF16)]
        + scratch_y
        + [
            pltpu.VMEM(light_field.shape, F32),
            pltpu.VMEM((2, times, across, width_y), F32),
            pltpu.VMEM(phase_y.shape, F32),
            pltpu.VMEM(sent_shape, F32),
            pltpu.SemaphoreType.DMA((1 + across // min(16, across),)),
        ],
    )
    received = exchange(sent)
    cells = (width_x, width)
    field, growth, gained, theirs = call(
        second_kernel,
        put(table_x, density_y, *received),
        vmem((2, total) + cells, (total,) + cells, (total,) + cells, (blocks, 2, width_x // 2, width)),
        [pltpu.VMEM(sent_shape, F32)] + scratch_x,
    )
    kept, given = entering_density(growth, gained, theirs, True)
    (table_y,) = call(
        functools.partial(table_kernel, 1), put(phase_y, theirs), [(table_y_shape, BF16, VMEM_SPEC)]
    )
    table_y, given = lax.optimization_barrier((table_y, given))
    sent = call(
        third_kernel,
        put(field, growth, gained, table_x, kept, given),
        vmem(*[piece] * slabs),
        [pltpu.VMEM((blocks,) + cells, F32)] + scratch_x + [pltpu.VMEM(sent_shape, F32)],
    )
    received = exchange(sent)
    cells = (across, width_y)
    field, growth, gained, theirs = call(
        fourth_kernel,
        put(table_y, density_x, *received),
        vmem((2, times) + cells, (times,) + cells, (times,) + cells, (1, 2, across // 2, width_y)),
        [pltpu.VMEM(sent_shape, F32)] + scratch_y,
    )
    kept, given = entering_density(growth, gained, theirs, False)
    rows = across // 2
    light_half, electrons_half = (2, rows, times, width_y), (rows, times, width_y)
    own = call(own_kernel, put(field, growth, gained, kept), vmem(light_half, electrons_half))
    return call(
        other_kernel,
        put(field, growth, gained, given, *own),
        [(light_field.shape, F32, HBM_SPEC), ((across, times, width_y), F32, HBM_SPEC)],
        [
            pltpu.VMEM(light_half, F32),
            pltpu.VMEM(electrons_half, F32),
            pltpu.SemaphoreType.DMA((2, 1 + rows // min(8, rows))),
        ],
    )


def solution(mesh):
    slabs, trans = mesh.shape["tm"], mesh.shape["trans"]
    split = Mesh(mesh.devices.reshape(slabs // 4, 2, 2, trans), ("zh", "zl", "core", "trans"))
    time_axes = ("zh", "zl", "core")
    return jax.shard_map(
        local,
        mesh=split,
        in_specs=(P(None, "trans", time_axes, None), P(), P(), P()),
        out_specs=(P(None, "trans", time_axes, None), P("trans", time_axes, None)),
        check_vma=False,
    )
```

```python
import functools
import math

import jax
import jax.numpy as jnp
from jax import lax
from jax.experimental import pallas as pl
from jax.experimental.pallas import tpu as pltpu
from jax.sharding import Mesh
from jax.sharding import PartitionSpec as P

PHOTONS = 8
STEPS = 2
RATE_COEF = 1.8e-08
RECOMB = 0.02
KERR_COEF = 0.3
PLASMA = 4.0
LANES = 128
Z_AXES = ("zh", "zl")
GROUP = ("zl", "trans")
VMEM_LIMIT = 16 * 1024 * 1024
F32 = jnp.float32
BF16 = jnp.bfloat16
VMEM_SPEC = pl.BlockSpec(memory_space=pltpu.VMEM)
ANY_SPEC = pl.BlockSpec(memory_space=pl.ANY)
HBM_SPEC = pl.BlockSpec(memory_space=pltpu.MemorySpace.HBM)


def sincos(quarter):
    turns = jnp.floor(quarter * (2.0 / math.pi) + 0.5)
    rest = quarter - turns * 1.5703125
    rest = rest - turns * 4.837512969970703125e-4
    rest = rest - turns * 7.54978995489188e-8
    square = rest * rest
    sine = ((-1.9515295891e-4 * square + 8.3321608736e-3) * square - 1.6666654611e-1) * square
    sine = sine * rest + rest
    cosine = (2.443315711809948e-5 * square - 1.388731625493765e-3) * square
    cosine = (cosine + 4.166664568298827e-2) * (square * square) - 0.5 * square + 1.0
    for _ in range(2):
        twice = sine + sine
        sine, cosine = twice * cosine, 1.0 - twice * sine
    return sine, cosine


def split3(value):
    high = value.astype(BF16)
    rest = value - high.astype(F32)
    middle = rest.astype(BF16)
    low = (rest - middle.astype(F32)).astype(BF16)
    return high, middle, low


def turned(value, order, position, sign):
    re, im = value
    eighth = (position * 8) // order
    if (position * 8) % order == 0 and eighth % 2 == 0:
        quarter = (eighth // 2 * sign) % 4
        return ((re, im), (-im, re), (-re, -im), (im, -re))[quarter]
    angle = sign * 2.0 * math.pi * position / order
    c, s = math.cos(angle), math.sin(angle)
    if (position * 8) % order == 0:
        root = math.sqrt(0.5)
        sc, ss = math.copysign(1, c), math.copysign(1, s)
        one = re - im if sc == ss else re + im
        two = re + im if sc == ss else re - im
        new_re = one * (root * sc)
        new_im = two * (root * ss) if sc == ss else two * (root * ss)
        return (new_re, new_im)
    return (re * c - im * s, re * s + im * c)


def small_dft(values, sign):
    count = len(values)
    if count == 1:
        return values
    even = small_dft(values[0::2], sign)
    odd = small_dft(values[1::2], sign)
    upper, lower = [], []
    for k in range(count // 2):
        other = turned(odd[k], count, k, sign)
        upper.append((even[k][0] + other[0], even[k][1] + other[1]))
        lower.append((even[k][0] - other[0], even[k][1] - other[1]))
    return upper + lower


def ionise(re, im, density):
    intensity = re * re + im * im
    power = intensity * intensity
    power = power * power
    rate = RATE_COEF * (power * power)
    loss = rate + RECOMB
    decay = jnp.exp(-loss)
    source = (1.0 - decay) * density * rate / loss
    return decay, source


def rotate(re, im, electrons):
    intensity = re * re + im * im
    sine, cosine = sincos((0.25 * KERR_COEF) * intensity - (0.25 * PLASMA) * electrons)
    return re * cosine - im * sine, re * sine + im * cosine


def wave(shape, order, sign):
    product = lax.broadcasted_iota(jnp.int32, shape, 0) * lax.broadcasted_iota(jnp.int32, shape, 1)
    sine, cosine = sincos((product % order).astype(F32) * (0.5 * math.pi / order))
    return cosine, sign * sine


def toeplitz_blocks(phase, radix, sign):
    length = radix * LANES
    waves = jnp.concatenate(wave((LANES, LANES), length, sign), axis=1)
    block_re, block_im = wave((radix, LANES), radix, sign)
    block_re, block_im = block_re * (1.0 / length), block_im * (1.0 / length)
    sine, cosine = sincos(0.25 * phase)
    lane = lax.broadcasted_iota(jnp.int32, phase.shape, 1) % radix
    picked = [jnp.where(lane == k, part, 0.0) for part in (cosine, sine) for k in range(radix)]
    spectrum = jnp.dot(
        jnp.concatenate(picked, axis=0),
        waves,
        precision=lax.Precision.HIGHEST,
        preferred_element_type=F32,
    )
    half = radix * radix
    row = lax.broadcasted_iota(jnp.int32, (LANES, LANES), 0)
    column = lax.broadcasted_iota(jnp.int32, (LANES, LANES), 1)
    direct = column >= row
    blocks = []
    for k in range(radix):
        ours = slice(k * radix, (k + 1) * radix)
        theirs = slice(half + k * radix, half + (k + 1) * radix)
        re = spectrum[ours, :LANES] - spectrum[theirs, LANES:]
        im = spectrum[ours, LANES:] + spectrum[theirs, :LANES]
        full_re = jnp.sum(re * block_re - im * block_im, axis=0, keepdims=True)
        full_im = jnp.sum(re * block_im + im * block_re, axis=0, keepdims=True)
        spread_re = jnp.broadcast_to(full_re, (LANES, LANES))
        spread_im = jnp.broadcast_to(full_im, (LANES, LANES))
        rolled = (
            pltpu.roll(spread_re, 0, 1, stride=1, stride_axis=0),
            pltpu.roll(spread_im, 0, 1, stride=1, stride_axis=0),
        )
        wrapped = turned(rolled, radix, k, -sign)
        blocks.append(
            (jnp.where(direct, rolled[0], wrapped[0]), jnp.where(direct, rolled[1], wrapped[1]))
        )
    return blocks


def store_parts(table_ref, blocks):
    for k, (re, im) in enumerate(blocks):
        for part, (a, b) in enumerate(zip(split3(re), split3(im), strict=True)):
            table_ref[k, part, 0] = a
            table_ref[k, part, 1] = b


def table_kernel(sign, phase_ref, *refs):
    table_ref = refs[-1]
    store_parts(table_ref, toeplitz_blocks(phase_ref[...], table_ref.shape[0], sign))


def forward_y(load, start, step, radix, parts_ref):
    blocks = small_dft([load(a) for a in range(radix)], -1)
    for k, (re, im) in enumerate(blocks):
        for part, (a, b) in enumerate(zip(split3(re), split3(im), strict=True)):
            parts_ref[k, part, start : start + step, :LANES] = a
            parts_ref[k, part, start : start + step, LANES:] = b


def product_y(parts_ref, table_ref, out_ref, radix):
    for k in range(radix):
        high, middle, low = parts_ref[k, 0], parts_ref[k, 1], parts_ref[k, 2]
        left = jnp.concatenate([high, high, high, middle, middle, low], axis=1)
        rights = []
        for part in range(3):
            re, im = table_ref[k, part, 0], table_ref[k, part, 1]
            rights.append(jnp.concatenate([re, im], axis=1))
            rights.append(jnp.concatenate([-im, re], axis=1))
        right = jnp.concatenate(rights + rights[:4] + rights[:2], axis=0)
        out_ref[k] = jnp.dot(left, right, preferred_element_type=F32)


def backward_y(out_ref, start, step, radix):
    picked = [
        (out_ref[k, start : start + step, :LANES], out_ref[k, start : start + step, LANES:])
        for k in range(radix)
    ]
    return small_dft(picked, 1)


def member_and_flip(slabs):
    turned_pair = lax.rem(lax.axis_index("zh"), 2)
    return lax.axis_index(GROUP), turned_pair * (slabs // 2)


def give_out(send_ref, out_refs, flip):
    member, _ = member_and_flip(len(out_refs))
    for k, out_ref in enumerate(out_refs):
        out_ref[...] = send_ref[member ^ k ^ flip]


def take_in(recv_ref, in_refs, flip):
    member, _ = member_and_flip(len(in_refs))
    for k, in_ref in enumerate(in_refs):
        recv_ref[member ^ k ^ flip] = in_ref[...]


def first_kernel(light_hbm, phase_hbm, *refs):
    out_refs = refs[:-8]
    table_ref, parts_ref, mid_ref, light_ref, rows_ref, phase_ref, send_ref, sem = refs[-8:]
    radix = table_ref.shape[0]
    _, across, times, _ = light_ref.shape
    width = send_ref.shape[-1]
    step = min(32, across)
    chunks = range(0, across, step)
    phase_copy = pltpu.make_async_copy(phase_hbm, phase_ref, sem.at[0])
    phase_copy.start()
    arriving = []
    for i, x in enumerate(chunks):
        rows = pl.ds(x, step)
        copy = pltpu.make_async_copy(light_hbm.at[:, rows], light_ref.at[:, rows], sem.at[1 + i])
        copy.start()
        arriving.append(copy)
    phase_copy.wait()
    store_parts(table_ref, toeplitz_blocks(phase_ref[...], radix, 1))
    for copy, x in zip(arriving, chunks, strict=True):
        copy.wait()
        for t in range(times):
            for c in range(2):
                for start in range(x, x + step, 8):
                    rows_ref[c, t, start : start + 8, :] = light_ref[c, start : start + 8, t, :]

            def load(a, x=x, t=t):
                lanes = slice(a * LANES, (a + 1) * LANES)
                rows = slice(x, x + step)
                return rows_ref[0, t, rows, lanes], rows_ref[1, t, rows, lanes]

            forward_y(load, t * across + x, step, radix, parts_ref)
    product_y(parts_ref, table_ref, mid_ref, radix)
    for t in range(times):
        for x in range(0, across, 8):
            rows = slice(x, x + 8)
            for a, pair in enumerate(backward_y(mid_ref, t * across + x, 8, radix)):
                for c in range(2):
                    if width >= LANES:
                        slab, offset = a * LANES // width, a * LANES % width
                        send_ref[slab, c, t, rows, offset : offset + LANES] = pair[c]
                    else:
                        for piece in range(LANES // width):
                            slab = a * LANES // width + piece
                            lanes = slice(piece * width, (piece + 1) * width)
                            send_ref[slab, c, t, rows, :] = pair[c][:, lanes]
    give_out(send_ref, out_refs, member_and_flip(len(out_refs))[1])


def put_x(parts_ref, lanes, start, values):
    step = values[0][0].shape[0]
    for k, (re, im) in enumerate(small_dft(values, -1)):
        for part, (a, b) in enumerate(zip(split3(re), split3(im), strict=True)):
            base = part * 2 * LANES
            parts_ref[k, base + start : base + start + step, lanes] = a
            parts_ref[k, base + LANES + start : base + LANES + start + step, lanes] = b


def product_x(parts_ref, table_ref, out_ref, radix):
    for k in range(radix):
        lefts = []
        for part in range(3):
            re, im = table_ref[k, part, 0], table_ref[k, part, 1]
            lefts.append(jnp.concatenate([re, im], axis=0))
            lefts.append(jnp.concatenate([-im, re], axis=0))
        left = jnp.concatenate(lefts + lefts[:4] + lefts[:2], axis=1)
        high = parts_ref[k, : 2 * LANES]
        middle = parts_ref[k, 2 * LANES : 4 * LANES]
        low = parts_ref[k, 4 * LANES :]
        right = jnp.concatenate([high, high, high, middle, middle, low], axis=0)
        out_ref[k] = jnp.dot(left, right, preferred_element_type=F32)


def get_x(out_ref, lanes, start, step, radix):
    picked = [
        (out_ref[k, start : start + step, lanes], out_ref[k, LANES + start : LANES + start + step, lanes])
        for k in range(radix)
    ]
    return small_dft(picked, 1)


def second_kernel(table_ref, density_ref, *refs):
    in_refs = refs[:-7]
    field_ref, growth_ref, gained_ref, theirs_ref, recv_ref, parts_ref, mid_ref = refs[-7:]
    radix = table_ref.shape[0]
    sources, _, times, across, width = recv_ref.shape
    trans = (radix * LANES) // across
    step = min(16, across)
    total = (sources // trans) * times
    take_in(recv_ref, in_refs, 0)

    def at(c, t, x):
        place, inner = t // times, t % times
        return recv_ref[place * trans + x // across, c, inner, x % across : x % across + step, :]

    for t in range(total):
        lanes = slice(t * width, (t + 1) * width)
        for start in range(0, LANES, step):
            values = [
                (at(0, t, a * LANES + start), at(1, t, a * LANES + start)) for a in range(radix)
            ]
            put_x(parts_ref, lanes, start, values)
    product_x(parts_ref, table_ref, mid_ref, radix)
    for start in range(0, LANES, 8):
        carry = [None] * radix
        for t in range(total):
            lanes = slice(t * width, (t + 1) * width)
            for a, (re, im) in enumerate(get_x(mid_ref, lanes, start, 8, radix)):
                rows = slice(a * LANES + start, a * LANES + start + 8)
                field_ref[0, t, rows, :] = re
                field_ref[1, t, rows, :] = im
                growth, gained = ionise(re, im, density_ref[rows, :])
                if t % times:
                    gained = growth * carry[a][1] + gained
                    growth = growth * carry[a][0]
                growth_ref[t, rows, :] = growth
                gained_ref[t, rows, :] = gained
                carry[a] = (growth, gained)
    hand_partner(growth_ref, gained_ref, theirs_ref)


def third_kernel(field_ref, growth_ref, gained_ref, table_ref, kept_ref, given_ref, *refs):
    out_refs = refs[:-4]
    entering_ref, parts_ref, mid_ref, send_ref = refs[-4:]
    radix = table_ref.shape[0]
    _, total, _, width = field_ref.shape
    slabs, _, times, across, _ = send_ref.shape
    trans = (radix * LANES) // across
    half = radix * LANES // 2
    core = lax.axis_index("core")
    entering_ref[:, pl.ds(pl.multiple_of(core * half, 8), half)] = kept_ref[...]
    entering_ref[:, pl.ds(pl.multiple_of((1 - core) * half, 8), half)] = given_ref[...]
    step = 16
    for start in range(0, LANES, step):
        for t in range(total):
            lanes = slice(t * width, (t + 1) * width)
            values = []
            for a in range(radix):
                rows = slice(a * LANES + start, a * LANES + start + step)
                electrons = growth_ref[t, rows, :] * entering_ref[t // times, rows, :] + gained_ref[t, rows, :]
                values.append(rotate(field_ref[0, t, rows, :], field_ref[1, t, rows, :], electrons))
            put_x(parts_ref, lanes, start, values)
    product_x(parts_ref, table_ref, mid_ref, radix)
    for t in range(total):
        lanes = slice(t * width, (t + 1) * width)
        place, inner = t // times, t % times
        for start in range(0, LANES, 8):
            for a, pair in enumerate(get_x(mid_ref, lanes, start, 8, radix)):
                x = a * LANES + start
                row = x % across
                for c in range(2):
                    send_ref[place * trans + x // across, c, inner, row : row + 8, :] = pair[c]
    give_out(send_ref, out_refs, 0)


def fourth_kernel(table_ref, density_ref, *refs):
    in_refs = refs[:-7]
    field_ref, growth_ref, gained_ref, theirs_ref, recv_ref, parts_ref, mid_ref = refs[-7:]
    radix = table_ref.shape[0]
    _, times, across, _ = field_ref.shape
    width = recv_ref.shape[-1]
    step = min(16, across)
    take_in(recv_ref, in_refs, member_and_flip(len(in_refs))[1])

    def part(c, t, x, a):
        rows = slice(x, x + step)
        if width >= LANES:
            slab, offset = a * LANES // width, a * LANES % width
            return recv_ref[slab, c, t, rows, offset : offset + LANES]
        pieces = LANES // width
        return jnp.concatenate(
            [recv_ref[a * pieces + p, c, t, rows, :] for p in range(pieces)], axis=1
        )

    for x in range(0, across, step):
        for t in range(times):

            def load(a, x=x, t=t):
                return part(0, t, x, a), part(1, t, x, a)

            forward_y(load, t * across + x, step, radix, parts_ref)
    product_y(parts_ref, table_ref, mid_ref, radix)
    for x in range(0, across, 8):
        rows = slice(x, x + 8)
        carry = [None] * radix
        for t in range(times):
            for a, (re, im) in enumerate(backward_y(mid_ref, t * across + x, 8, radix)):
                lanes = slice(a * LANES, (a + 1) * LANES)
                field_ref[0, t, rows, lanes] = re
                field_ref[1, t, rows, lanes] = im
                growth, gained = ionise(re, im, density_ref[rows, lanes])
                if t:
                    gained = growth * carry[a][1] + gained
                    growth = growth * carry[a][0]
                growth_ref[t, rows, lanes] = growth
                gained_ref[t, rows, lanes] = gained
                carry[a] = (growth, gained)
    hand_partner(growth_ref, gained_ref, theirs_ref)


def last_maps(growth_ref, gained_ref, blocks, half, side):
    times = growth_ref.shape[0] // blocks
    rows = pl.ds(pl.multiple_of(side * half, 8), half)
    ends = [block * times + times - 1 for block in range(blocks)]
    return [(growth_ref[t, rows, :], gained_ref[t, rows, :]) for t in ends]


def hand_partner(growth_ref, gained_ref, theirs_ref):
    blocks, _, half, _ = theirs_ref.shape
    core = lax.axis_index("core")
    for block, maps in enumerate(last_maps(growth_ref, gained_ref, blocks, half, 1 - core)):
        for i in range(2):
            theirs_ref[block, i] = maps[i]


def in_order(growth_ref, gained_ref, other_ref):
    blocks, _, half, _ = other_ref.shape
    core = lax.axis_index("core")
    first = core == 0
    ordered = []
    for block, maps in enumerate(last_maps(growth_ref, gained_ref, blocks, half, core)):
        other = other_ref[block, 0], other_ref[block, 1]
        ordered.append([jnp.where(first, a, b) for a, b in zip(maps, other, strict=True)])
        ordered.append([jnp.where(first, b, a) for a, b in zip(maps, other, strict=True)])
    return ordered


def whole_map_kernel(growth_ref, gained_ref, other_ref, out_gained_ref, out_growth_ref=None):
    growth, gained = None, None
    for a, b in in_order(growth_ref, gained_ref, other_ref):
        growth, gained = (a, b) if growth is None else (growth * a, a * gained + b)
    out_gained_ref[...] = gained
    if out_growth_ref is not None:
        out_growth_ref[...] = growth


def hand_over_kernel(paired, rebuild, growth_ref, gained_ref, other_ref, *refs):
    kept_ref, given_ref = refs[-2:]
    entering = finish_scan(Z_AXES, rebuild([ref[...] for ref in refs[:-2]]), paired)
    before = []
    for a, b in in_order(growth_ref, gained_ref, other_ref):
        before.append(entering)
        entering = a * entering + b
    first = lax.axis_index("core") == 0
    for block in range(kept_ref.shape[0]):
        early, late = before[2 * block : 2 * block + 2]
        kept_ref[block] = jnp.where(first, early, late)
        given_ref[block] = jnp.where(first, late, early)


def turn_rows(base, x, field_ref, growth_ref, gained_ref, entering_ref, light_ref, electrons_ref):
    _, times, _, length = field_ref.shape
    rows, out_rows = pl.ds(pl.multiple_of(base + x, 8), 8), slice(x, x + 8)
    entering = entering_ref[0, out_rows, :]
    for t in range(times):
        results = []
        for a in range(length // LANES):
            lanes = slice(a * LANES, (a + 1) * LANES)
            electrons = growth_ref[t, rows, lanes] * entering[:, lanes] + gained_ref[t, rows, lanes]
            re, im = rotate(field_ref[0, t, rows, lanes], field_ref[1, t, rows, lanes], electrons)
            results.append((re, im, electrons))
        re, im, electrons = (jnp.concatenate(part, axis=1) for part in zip(*results, strict=True))
        light_ref[0, out_rows, t, :] = re
        light_ref[1, out_rows, t, :] = im
        electrons_ref[out_rows, t, :] = electrons


def own_kernel(field_ref, growth_ref, gained_ref, entering_ref, light_ref, electrons_ref):
    half = field_ref.shape[2] // 2
    base = lax.axis_index("core") * half
    for x in range(0, half, 8):
        turn_rows(base, x, field_ref, growth_ref, gained_ref, entering_ref, light_ref, electrons_ref)


def other_kernel(
    field_ref, growth_ref, gained_ref, entering_ref, own_light_ref, own_electrons_ref, light_hbm, electrons_hbm,
    light_ref, electrons_ref, sem,
):
    half = field_ref.shape[2] // 2
    core = lax.axis_index("core")
    base = (1 - core) * half
    leaving = []

    def leave(i, light, electrons, target):
        for copy in (
            pltpu.make_async_copy(light, light_hbm.at[:, target], sem.at[0, i]),
            pltpu.make_async_copy(electrons, electrons_hbm.at[target], sem.at[1, i]),
        ):
            copy.start()
            leaving.append(copy)

    leave(0, own_light_ref, own_electrons_ref, pl.ds(core * half, half))
    step = min(16, half)
    for i, begin in enumerate(range(0, half, step)):
        for x in range(begin, begin + step, 8):
            turn_rows(base, x, field_ref, growth_ref, gained_ref, entering_ref, light_ref, electrons_ref)
        block = pl.ds(begin, step)
        leave(1 + i, light_ref.at[:, block], electrons_ref.at[block], pl.ds(base + begin, step))
    for copy in leaving:
        copy.wait()


def call(kernel, operands, outs, scratch=()):
    return pl.pallas_call(
        kernel,
        out_shape=[jax.ShapeDtypeStruct(shape, kind) for shape, kind, _ in outs],
        in_specs=[spec for _, spec in operands],
        out_specs=[spec for _, _, spec in outs],
        scratch_shapes=list(scratch),
        compiler_params=pltpu.CompilerParams(vmem_limit_bytes=VMEM_LIMIT),
    )(*[array for array, _ in operands])


def in_hbm(array):
    return pltpu.with_memory_space_constraint(array, pltpu.MemorySpace.HBM)


def fuse(function, *arrays):
    outs = jax.eval_shape(function, *arrays)

    def kernel(*refs):
        results = function(*[ref[...] for ref in refs[: len(arrays)]])
        for ref, result in zip(refs[len(arrays) :], results, strict=True):
            ref[...] = result

    return call(
        kernel,
        [(array, VMEM_SPEC) for array in arrays],
        [(out.shape, out.dtype, VMEM_SPEC) for out in outs],
    )


def widen(pairs):
    return [(2 * a + i, 2 * b + (i + a + b) % 2) for a, b in pairs for i in range(2)]


def scan_levels(axis, gained, growth, paired):
    count = lax.axis_size(axis) // (2 if paired else 1)
    levels = []
    size = 1
    while size < count:
        pairs = [(i, i // (2 * size) * 2 * size + 2 * size - 1 - i % (2 * size)) for i in range(count)]
        pairs = widen(pairs) if paired else pairs
        got = [lax.ppermute(gained, axis, pairs)]
        if 2 * size < count:
            got.append(lax.ppermute(growth, axis, pairs))

            def join(growth, gained, got_gained, got_growth, size=size):
                upper = (lax.axis_index(axis) // (2 if paired else 1) // size) % 2 == 1
                later_growth = jnp.where(upper, growth, got_growth)
                early, late = jnp.where(upper, got_gained, gained), jnp.where(upper, gained, got_gained)
                results = (later_growth * early + late, growth * got_growth)
                return results if 4 * size < count else results[:1]

            gained, *rest = fuse(join, growth, gained, *got)
            growth = rest[0] if rest else None
        levels.append(got)
        size *= 2
    return levels


def finish_scan(axis, levels, paired):
    place = lax.axis_index(axis) // (2 if paired else 1)
    before_growth = before_gained = None
    for level, got in enumerate(levels):
        upper = (place // 2**level) % 2 == 1
        new_gained = got[0]
        if before_gained is None:
            before_gained = jnp.where(upper, new_gained, 0.0)
        else:
            new_gained = before_growth * new_gained + before_gained
            before_gained = jnp.where(upper, new_gained, before_gained)
        if len(got) > 1:
            new_growth = got[1] if before_growth is None else before_growth * got[1]
            before_growth = jnp.where(upper, new_growth, 1.0 if before_growth is None else before_growth)
    return before_gained


def flatten(levels):
    leaves, tree = jax.tree.flatten(levels)
    return leaves, lambda values: jax.tree.unflatten(tree, values)


def swap_cores(array):
    return lax.ppermute(array, "core", [(0, 1), (1, 0)])


def exchange(blocks):
    count = len(blocks)
    moved = {
        k: lax.ppermute(blocks[k], GROUP, [(m, m ^ k) for m in range(count)])
        for k in range(count - 1, 0, -1)
    }
    return [blocks[0]] + [moved[k] for k in range(1, count)]


def entering_density(growth, gained, theirs, paired):
    blocks, _, half, lanes = theirs.shape
    other = swap_cores(theirs)
    maps = [(array, VMEM_SPEC) for array in (growth, gained, other)]
    one = ((half, lanes), F32, VMEM_SPEC)
    single = lax.axis_size(Z_AXES) // (2 if paired else 1) <= 2
    whole = call(whole_map_kernel, maps, [one] if single else [one, one])
    levels = scan_levels(Z_AXES, whole[0], None if single else whole[1], paired)
    leaves, rebuild = flatten(levels)
    both = ((blocks, half, lanes), F32, VMEM_SPEC)
    kept, given = call(
        functools.partial(hand_over_kernel, paired, rebuild),
        maps + [(leaf, VMEM_SPEC) for leaf in leaves],
        [both, both],
    )
    return kept, swap_cores(given)


def local(light_field, gas_density, phase_x, phase_y):
    width_x, width_y = phase_x.shape[0], phase_y.shape[0]
    radix_x, radix_y = width_x // LANES, width_y // LANES
    _, across, times, _ = light_field.shape
    trans, slabs = lax.axis_size("trans"), lax.axis_size(GROUP)
    blocks = slabs // trans
    width = width_y // slabs
    member, flip = member_and_flip(slabs)
    density_y = lax.dynamic_slice_in_dim(gas_density, (member ^ flip) * width, width, 1)
    density_x = lax.dynamic_slice_in_dim(gas_density, lax.axis_index("trans") * across, across, 0)
    density_y, density_x = lax.optimization_barrier((density_y, density_x))
    piece = (2, times, across, width)
    sent_shape = (slabs,) + piece
    total = blocks * times
    rows = times * across

    def vmem(*shapes):
        return [(shape, F32, VMEM_SPEC) for shape in shapes]

    def put(*arrays):
        return [(array, VMEM_SPEC) for array in arrays]

    scratch_y = [
        pltpu.VMEM((radix_y, 3, rows, 2 * LANES), BF16),
        pltpu.VMEM((radix_y, rows, 2 * LANES), F32),
    ]
    scratch_x = [
        pltpu.VMEM((radix_x, 6 * LANES, total * width), BF16),
        pltpu.VMEM((radix_x, 2 * LANES, total * width), F32),
    ]
    table_y_shape = (radix_y, 3, 2, LANES, LANES)
    phase_y = phase_y.reshape(radix_y, LANES)
    (table_x,) = call(
        functools.partial(table_kernel, -1),
        put(phase_x.reshape(radix_x, LANES)),
        [((radix_x, 3, 2, LANES, LANES), BF16, VMEM_SPEC)],
    )
    sent = call(
        first_kernel,
        [(in_hbm(light_field), HBM_SPEC), (in_hbm(phase_y), HBM_SPEC)],
        vmem(*[piece] * slabs),
        [pltpu.VMEM(table_y_shape, BF16)]
        + scratch_y
        + [
            pltpu.VMEM(light_field.shape, F32),
            pltpu.VMEM((2, times, across, width_y), F32),
            pltpu.VMEM(phase_y.shape, F32),
            pltpu.VMEM(sent_shape, F32),
            pltpu.SemaphoreType.DMA((1 + across // min(32, across),)),
        ],
    )
    received = exchange(sent)
    cells = (width_x, width)
    field, growth, gained, theirs = call(
        second_kernel,
        put(table_x, density_y, *received),
        vmem((2, total) + cells, (total,) + cells, (total,) + cells, (blocks, 2, width_x // 2, width)),
        [pltpu.VMEM(sent_shape, F32)] + scratch_x,
    )
    kept, given = entering_density(growth, gained, theirs, True)
    sent = call(
        third_kernel,
        put(field, growth, gained, table_x, kept, given),
        vmem(*[piece] * slabs),
        [pltpu.VMEM((blocks,) + cells, F32)] + scratch_x + [pltpu.VMEM(sent_shape, F32)],
    )
    (table_y,) = call(
        functools.partial(table_kernel, 1), put(phase_y, sent[0]), [(table_y_shape, BF16, VMEM_SPEC)]
    )
    received = exchange(sent)
    cells = (across, width_y)
    field, growth, gained, theirs = call(
        fourth_kernel,
        put(table_y, density_x, *received),
        vmem((2, times) + cells, (times,) + cells, (times,) + cells, (1, 2, across // 2, width_y)),
        [pltpu.VMEM(sent_shape, F32)] + scratch_y,
    )
    kept, given = entering_density(growth, gained, theirs, False)
    rows = across // 2
    light_half, electrons_half = (2, rows, times, width_y), (rows, times, width_y)
    own = call(own_kernel, put(field, growth, gained, kept), vmem(light_half, electrons_half))
    return call(
        other_kernel,
        put(field, growth, gained, given, *own),
        [(light_field.shape, F32, HBM_SPEC), ((across, times, width_y), F32, HBM_SPEC)],
        [
            pltpu.VMEM(light_half, F32),
            pltpu.VMEM(electrons_half, F32),
            pltpu.SemaphoreType.DMA((2, 1 + rows // min(16, rows))),
        ],
    )


def solution(mesh):
    slabs, trans = mesh.shape["tm"], mesh.shape["trans"]
    split = Mesh(mesh.devices.reshape(slabs // 4, 2, 2, trans), ("zh", "zl", "core", "trans"))
    time_axes = ("zh", "zl", "core")
    return jax.shard_map(
        local,
        mesh=split,
        in_specs=(P(None, "trans", time_axes, None), P(), P(), P()),
        out_specs=(P(None, "trans", time_axes, None), P("trans", time_axes, None)),
        check_vma=False,
    )
```
